32 devices in a mesh: region: 8 (over z, core), member: 4 (over y, x).
Axes of the slice: x: 2, y: 2, z: 4, core: 2. Of those that a mesh axis runs over, the one named last changes fastest.
Arguments:
- positions: float32 [3, 12288], P(None, ('region', 'member'))
- forces: float32 [3, 12288], P(None, ('region', 'member')), may hold values from -6 to 6
- blob_platelet: int32 [12288], P(('region', 'member')), may hold values from 0 to 8, as said below
- blob_rank: int32 [12288], P(('region', 'member')), may hold values from 0 to 161, as said below
- platelet_owner: int32 [64], P('region'), may hold values from 0 to 7, as said below
- pair_list: int32 [96, 8], P(('region', 'member')), may hold values from 0 to 23, as said below
- pair_count: int32 [96], P(('region', 'member')), may hold values from 1 to 8, as said below
- preconditioner: bfloat16 [64, 486, 486], P(('region', 'member')), may hold values from -0.25 to 0.25
Outputs:
- blob_velocity: float32 [3, 12288], P(None, ('region', 'member'))
- body_velocity: float32 [64, 486], P(('region', 'member'))
The draws below stay inside these ranges and needn't reach their ends.
Inputs may be any that keep to these rules, and one draw needn't show every extreme that they name: `blob_platelet`: in each slab every platelet id below 8 appears on exactly 162 slots, and 8 marks an empty slot. Every device holds exactly 324 live blobs, of which at most 121 belong to platelets whose owner slots lie on one member; that bound is met in every slab. `blob_rank`: the 162 blobs of one platelet have distinct ranks; empty slots have rank 0. `platelet_owner`: the 8 entries of one slab are a permutation; owner slot o lies on member o // 2 of that slab. `pair_list`: the entries of one target tile are distinct, and entry 0 is the tile itself, 6 plus its index within its slab. `pair_count`: some tile has 8 in every draw.
All inputs are finite; a program needn't handle non-finite values.
Results may differ from the reference program's by a relative error of at most 0.0029.
Values sent between devices are 32-bit elements; how exact they have to be, the bound alone decides.
A program may use at most 64 MiB of HBM per device.

```python
import math
import jax
import jax.numpy as jnp
from jax import lax

TILE = 128
PB = 162
BODY = 486
PLAT_DEV = 2
PAIRS = 8
BLOB_DEV = 384
REG_BLK = 12
REG_BLOBS = 1536
EXT_BLK = 24
PLAT_REG = 8
NPLATS = 64
NBLOCKS = 96
NBLOBS = 12288
CAP = 121
N_REGION = 8
N_MEMBER = 4


slab_width = 2.0


span_width = 4.0


def region_layout(region_key):
    order_key, share_key, latin_key, shuffle_key = jax.random.split(region_key, 4)
    owner_map = jax.random.permutation(order_key, PLAT_REG).astype(jnp.int32)
    inverse_map = jnp.zeros((PLAT_REG,), jnp.int32).at[owner_map].set(jnp.arange(PLAT_REG, dtype=jnp.int32))
    total_live = PLAT_DEV * PB
    base_share = total_live // N_MEMBER
    leftover = total_live % N_MEMBER
    swings = jax.random.randint(share_key, (N_MEMBER // 2,), 0, base_share // 2 + 1).astype(jnp.int32)
    swings = swings.at[0].set(base_share // 2)
    paired = jnp.stack([swings, -swings], axis=1).reshape(N_MEMBER)
    shares = base_share + paired + (jnp.arange(N_MEMBER) < leftover).astype(jnp.int32)
    latin_shift = jax.random.permutation(latin_key, N_MEMBER).astype(jnp.int32)
    source_ids = jnp.arange(N_MEMBER, dtype=jnp.int32)
    grid_counts = shares[(source_ids[:, None] + latin_shift[None, :]) % N_MEMBER]
    grid_starts = jnp.cumsum(grid_counts, axis=0) - grid_counts
    offsets = jnp.arange(CAP, dtype=jnp.int32)
    is_valid = offsets[None, None, :] < grid_counts[:, :, None]
    within = grid_starts[:, :, None] + offsets[None, None, :]
    owner_member = jnp.broadcast_to(source_ids[None, :, None], is_valid.shape)
    width_all = N_MEMBER * CAP
    pad_valid = jnp.concatenate([is_valid.reshape(N_MEMBER, width_all), jnp.zeros((N_MEMBER, BLOB_DEV), jnp.bool_)], 1)
    pad_within = jnp.concatenate([within.reshape(N_MEMBER, width_all), jnp.zeros((N_MEMBER, BLOB_DEV), jnp.int32)], 1)
    pad_member = jnp.concatenate([owner_member.reshape(N_MEMBER, width_all), jnp.zeros((N_MEMBER, BLOB_DEV), jnp.int32)], 1)
    sort_key = jnp.where(pad_valid, 0, 1).astype(jnp.int32)
    chosen = jnp.argsort(sort_key, axis=1, stable=True)[:, :BLOB_DEV]
    scores = jax.random.randint(shuffle_key, (N_MEMBER, BLOB_DEV), 0, 2 ** 19) * BLOB_DEV + jnp.arange(BLOB_DEV, dtype=jnp.int32)[None, :]
    shuffle = jnp.argsort(scores, axis=1)
    picked = jnp.take_along_axis(chosen, shuffle, axis=1)
    slot_valid = jnp.take_along_axis(pad_valid, picked, axis=1)
    slot_within = jnp.take_along_axis(pad_within, picked, axis=1)
    slot_member = jnp.take_along_axis(pad_member, picked, axis=1)
    owner_slot = jnp.clip(slot_member * PLAT_DEV + slot_within // PB, 0, PLAT_REG - 1)
    plate_ids = jnp.where(slot_valid, inverse_map[owner_slot], PLAT_REG).astype(jnp.int32)
    rank_ids = jnp.where(slot_valid, slot_within % PB, 0).astype(jnp.int32)
    return (plate_ids.reshape(REG_BLOBS), rank_ids.reshape(REG_BLOBS), owner_map)


def layout_tables(key):
    region_keys = jax.random.split(jax.random.fold_in(key, 7), N_REGION)
    plate_ids, rank_ids, owner_maps = jax.vmap(region_layout)(region_keys)
    return (plate_ids.reshape(NBLOBS), rank_ids.reshape(NBLOBS), owner_maps.reshape(NPLATS))


def draw_blob_platelet(key, part):
    return layout_tables(key)[0]


def draw_blob_rank(key, part):
    return layout_tables(key)[1]


def draw_platelet_owner(key, part):
    return layout_tables(key)[2]


def draw_positions(key, part):
    uniforms = jax.random.uniform(key, (3, NBLOBS), jnp.float32)
    region_index = (jnp.arange(NBLOBS) // REG_BLOBS).astype(jnp.float32)
    height = 1.0 + 3.0 * uniforms[2]
    along = (region_index + uniforms[0]) * slab_width
    across = uniforms[1] * span_width
    return jnp.stack([along, across, height], 0).astype(jnp.float32)


def draw_pair_list(key, part):
    local_tile = jnp.arange(NBLOCKS, dtype=jnp.int32) % REG_BLK
    self_index = local_tile + REG_BLK // 2
    scores = jax.random.randint(key, (NBLOCKS, EXT_BLK - 1), 0, 2 ** 19) * EXT_BLK + jnp.arange(EXT_BLK - 1, dtype=jnp.int32)[None, :]
    chosen = jnp.argsort(scores, axis=1)[:, :PAIRS - 1] + 1
    others = (self_index[:, None] + chosen) % EXT_BLK
    return jnp.concatenate([self_index[:, None], others], 1).astype(jnp.int32)


def draw_pair_count(key, part):
    first_key, second_key = jax.random.split(key, 2)
    counts = jax.random.randint(first_key, (NBLOCKS,), 1, PAIRS + 1)
    marked = jax.random.randint(second_key, (), 0, NBLOCKS)
    return jnp.where(jnp.arange(NBLOCKS) == marked, PAIRS, counts).astype(jnp.int32)


def levels(rng, shape, pieces, least, top_value):
    level, own = 1.0, jax.random.fold_in(rng, 6)
    for axis_at, blocks in pieces:
        heights = jnp.exp(jax.random.uniform(jax.random.fold_in(own, axis_at), (blocks,), jnp.float32, least / len(pieces), top_value / len(pieces)))
        level = level * jnp.repeat(heights, shape[axis_at] // blocks).reshape([-1 if axis == axis_at else 1 for axis in range(len(shape))])
    return level


def noise(key, shape, deviation, bound, cuts=(), kind=jnp.bfloat16):
    values = deviation * jax.random.normal(key, shape, jnp.float32)
    if cuts:
        values = values * levels(key, shape, cuts, -0.22, 0.18)
    return jnp.clip(values, -bound, bound).astype(kind)


def setup_inputs(seed: int = 0) -> dict:
    key_list = jax.random.split(jax.random.key(seed), 9)
    positions = draw_positions(jax.random.fold_in(key_list[8], 71), 0)
    forces = noise(key_list[1], (3, NBLOBS), 1.0, 6.0, ((1, 32),), jnp.float32)
    blob_platelet = draw_blob_platelet(jax.random.fold_in(key_list[8], 71), 0)
    blob_rank = draw_blob_rank(jax.random.fold_in(key_list[8], 71), 0)
    platelet_owner = draw_platelet_owner(jax.random.fold_in(key_list[8], 71), 0)
    pair_list = draw_pair_list(jax.random.fold_in(key_list[8], 71), 0)
    pair_count = draw_pair_count(jax.random.fold_in(key_list[8], 71), 0)
    preconditioner = noise(key_list[7], (NPLATS, BODY, BODY), BODY ** -0.5, 0.25, ((0, 32),))
    return dict(positions=positions, forces=forces, blob_platelet=blob_platelet, blob_rank=blob_rank, platelet_owner=platelet_owner, pair_list=pair_list, pair_count=pair_count, preconditioner=preconditioner)


soft_square = 1.0

def stokes_sum(targets, sources, pushes):
    force = pushes[:, :, None, :]
    separation = targets[:, :, :, None] - sources[:, :, None, :]
    dist_square = lax.optimization_barrier(jnp.sum(separation * separation, axis=0))
    force_along = lax.optimization_barrier(jnp.sum(separation * force, axis=0))
    kernel_weight = 1.0 / (8.0 * math.pi * (dist_square + soft_square) * jnp.sqrt(dist_square + soft_square))
    direct = ((dist_square + 2.0 * soft_square) * force + separation * force_along) * kernel_weight
    flip_source = jnp.array([1.0, 1.0, -1.0], jnp.float32)[:, None, None]
    flip_pair = jnp.array([1.0, 1.0, -1.0], jnp.float32)[:, None, None, None]
    unit_normal = jnp.array([0.0, 0.0, 1.0], jnp.float32)[:, None, None, None]
    height = sources[2][:, None, :]
    image_gap = targets[:, :, :, None] - (sources * flip_source)[:, :, None, :]
    image_square = lax.optimization_barrier(jnp.sum(image_gap * image_gap, axis=0))
    inverse_one = 1.0 / jnp.sqrt(image_square)
    inverse_three = inverse_one * inverse_one * inverse_one
    inverse_five = inverse_three * inverse_one * inverse_one
    image_along = lax.optimization_barrier(jnp.sum(image_gap * force, axis=0))
    mirrored = force * flip_pair
    mirror_along = lax.optimization_barrier(jnp.sum(image_gap * mirrored, axis=0))
    normal_gap = image_gap[2]
    stokes_image = force * inverse_one + image_gap * image_along * inverse_three
    doublet = height * (mirrored * inverse_three - 3.0 * image_gap * mirror_along * inverse_five)
    doublet = doublet + unit_normal * mirror_along * inverse_three
    doublet = doublet - (mirrored * normal_gap + image_gap * mirrored[2]) * inverse_three
    doublet = doublet + 3.0 * image_gap * normal_gap * mirror_along * inverse_five
    wall_term = (2.0 * height * doublet - stokes_image) * (1.0 / (8.0 * math.pi))
    return lax.optimization_barrier(jnp.sum(direct + wall_term, axis=3))

def reference(positions, forces, blob_platelet, blob_rank, platelet_owner, pair_list, pair_count, preconditioner):
    live_mask = (blob_platelet < PLAT_REG).astype(jnp.float32)
    pushes = forces * live_mask[None, :]
    slab_data = jnp.concatenate([positions, pushes], 0).reshape(6, N_REGION, REG_BLOBS)
    half_width = REG_BLOBS // 2
    zero_rim = jnp.zeros((6, 1, half_width), jnp.float32)
    lower_rim = jnp.concatenate([zero_rim, slab_data[:, :-1, half_width:]], 1)
    upper_rim = jnp.concatenate([slab_data[:, 1:, :half_width], zero_rim], 1)
    extended = jnp.concatenate([lower_rim, slab_data, upper_rim], 2)
    extended = extended.reshape(6, N_REGION, EXT_BLK, TILE).transpose(1, 0, 2, 3)
    region_pairs = pair_list.reshape(N_REGION, REG_BLK, PAIRS)
    region_counts = pair_count.reshape(N_REGION, REG_BLK)

    def region_velocity(region_items):
        ext_region, pair_rows, count_rows = region_items
        targets = ext_region[:3, REG_BLK // 2:REG_BLK // 2 + REG_BLK]
        accumulated = jnp.zeros((3, REG_BLK, TILE), jnp.float32)
        for pair_slot in range(PAIRS):
            picked = jnp.take(ext_region, pair_rows[:, pair_slot], axis=1)
            keep_mask = (pair_slot < count_rows).astype(jnp.float32)
            accumulated = accumulated + keep_mask[None, :, None] * stokes_sum(targets, picked[:3], picked[3:])
        return accumulated
    velocity = lax.map(region_velocity, (extended, region_pairs, region_counts))
    blob_velocity = velocity.transpose(1, 0, 2, 3).reshape(3, NBLOBS)
    owner_rows = platelet_owner.reshape(N_REGION, PLAT_REG)
    plate_rows = blob_platelet.reshape(N_REGION, REG_BLOBS)
    rank_rows = blob_rank.reshape(N_REGION, REG_BLOBS)
    safe_plate = jnp.minimum(plate_rows, PLAT_REG - 1).astype(jnp.int32)
    slot_of = jnp.take_along_axis(owner_rows, safe_plate, axis=1)
    body_index = jnp.where(plate_rows < PLAT_REG, slot_of * PB + rank_rows, PLAT_REG * PB).astype(jnp.int32)
    region_vel = blob_velocity.reshape(3, N_REGION, REG_BLOBS).transpose(1, 0, 2)

    def place_body(region_items):
        velocity_rows, index_rows = region_items
        return jnp.zeros((3, PLAT_REG * PB), jnp.float32).at[:, index_rows].set(velocity_rows, mode='drop')
    body_flat = lax.map(place_body, (region_vel, body_index))
    body_in = body_flat.reshape(N_REGION, 3, PLAT_REG, PB).transpose(0, 2, 1, 3).reshape(NPLATS, BODY)
    body_in = body_in.astype(jnp.bfloat16)

    def apply_block(block_items):
        return jnp.dot(block_items[0], block_items[1], preferred_element_type=jnp.float32)
    body_velocity = lax.map(apply_block, (preconditioner, body_in))
    return (blob_velocity, body_velocity)
```

```python
import functools
import math

import jax
import jax.numpy as jnp
from jax import lax
from jax.experimental import pallas as pl
from jax.experimental.pallas import tpu as pltpu
from jax.sharding import PartitionSpec as P

TILE = 128
SUB = 8
VROWS = 4
ROWS = 6
SCALE = 1.0 / (8.0 * math.pi)
MESH = pl.DeviceIdType.MESH


def pair_terms(x1, x2, x3, src):
    y1, y2, h, f1, f2, f3, h2 = src
    d1 = x1 - y1
    d2 = x2 - y2
    d3 = x3 - h
    r3 = x3 + h
    s = d1 * d1 + d2 * d2
    w = lax.rsqrt(s + d3 * d3 + 1.0)
    p = lax.rsqrt(s + r3 * r3)
    w3 = w * w * w
    p2 = p * p
    p3 = p2 * p
    along = d1 * f1 + d2 * f2
    full = along + d3 * f3
    mirror = along - r3 * f3
    cp3 = (h2 * x3) * p3
    alpha = (w + w3) - (p + cp3)
    gamma = 3.0 * (cp3 * p2) * mirror
    both = full * (w3 - p3) + gamma
    return (
        f1 * alpha + d1 * both,
        f2 * alpha + d2 * both,
        f3 * alpha + d3 * both + h2 * gamma,
    )


def kernel(
    n_region,
    n_member,
    pb,
    own_plates,
    pos_hbm,
    force_hbm,
    plate_hbm,
    rank_hbm,
    owner_hbm,
    list_hbm,
    count_hbm,
    vel_out,
    body_out,
    pos,
    force,
    plate,
    rank,
    owner_ref,
    list_ref,
    count_ref,
    ext,
    ids,
    tgt,
    acc,
    vel,
    hot,
    local_sem,
    data_sem,
    vel_sem,
):
    r = lax.axis_index("region")
    m = lax.axis_index("member")
    half = n_member // 2
    tiles = pos.shape[1] // TILE
    blobs = pos.shape[1]
    plates = owner_ref.shape[0]
    pairs = list_ref.shape[1]
    has_low = r > 0
    has_high = r < n_region - 1
    to_high = jnp.logical_and(m >= half, has_high)
    to_low = jnp.logical_and(m < half, has_low)
    base = (half + m) * tiles

    def other(step):
        return lax.rem(m + step, n_member)

    barrier = pltpu.get_barrier_semaphore()
    for step in range(1, n_member):
        pl.semaphore_signal(barrier, inc=1, device_id=(r, other(step)), device_id_type=MESH)

    loads = [
        pltpu.make_async_copy(a, b, local_sem.at[i])
        for i, (a, b) in enumerate(
            ((pos_hbm, pos), (force_hbm, force), (plate_hbm, plate.at[0]), (rank_hbm, rank.at[0]),
             (owner_hbm, owner_ref), (list_hbm, list_ref), (count_hbm, count_ref))
        )
    ]
    for load in loads[:3]:
        load.start()

    @pl.when(has_low)
    def _():
        for k in range(half):
            pl.semaphore_signal(barrier, inc=1, device_id=(r - 1, half + k), device_id_type=MESH)

    @pl.when(has_high)
    def _():
        for k in range(half):
            pl.semaphore_signal(barrier, inc=1, device_id=(r + 1, k), device_id_type=MESH)

    for load in loads[3:]:
        load.start()

    for load in loads[:3]:
        load.wait()

    live = plate[...] < plates
    place_row = pos[...]
    push_row = force[...] * live.astype(jnp.float32)
    for t in range(tiles):
        span = slice(t * TILE, (t + 1) * TILE)
        for c in range(3):
            ext[base + t, c] = place_row[c : c + 1, span]
            ext[base + t, 3 + c] = push_row[c : c + 1, span]

    def block(e, count=1):
        return ext.at[pl.ds(e * tiles, count * tiles)]

    def move(src, dst, send, recv, to):
        return pltpu.make_async_remote_copy(
            src_ref=src, dst_ref=dst, send_sem=send, recv_sem=recv, device_id=to, device_id_type=MESH
        )

    def near_copy(step):
        here = block(half + m)
        return move(here, here, local_sem.at[0], data_sem.at[0], (r, other(step)))

    def rim_copy(k, shift, e, sem):
        return move(block(half + m), block(e), local_sem.at[1], data_sem.at[sem], (r + shift, lax.rem(m + k, n_member)))

    def sized(ref, send, recv):
        return move(ref, ref, send, recv, (r, other(1)))

    rim_sends = jnp.where(jnp.logical_or(to_high, to_low), n_member, 0)
    pl.semaphore_wait(barrier, n_member - 1 + rim_sends)

    for step in range(1, n_member):
        near_copy(step).start()

    @pl.when(to_high)
    def _():
        for k in range(n_member):
            rim_copy(k, 1, m - half, 1).start()

    @pl.when(to_low)
    def _():
        for k in range(n_member):
            rim_copy(k, -1, half + n_member + m, 2).start()

    for load in loads[3:]:
        load.wait()

    plate_row = plate[...]
    slot_of = jnp.zeros_like(plate_row)
    for k in range(plates):
        slot_of = jnp.where(plate_row == k, owner_ref[k], slot_of)
    body_at = jnp.where(live, slot_of * pb + rank[...], plates * pb)
    for t in range(tiles):
        ids[m * tiles + t] = body_at[:, t * TILE : (t + 1) * TILE]

    def ids_copy(step):
        here = ids.at[pl.ds(m * tiles, tiles)]
        return move(here, here, local_sem.at[2], data_sem.at[3], (r, other(step)))

    for step in range(1, n_member):
        ids_copy(step).start()

    @pl.when(jnp.logical_not(has_low))
    def _():
        ext[pl.ds(0, half * tiles)] = jnp.zeros((half * tiles, ROWS, 1, TILE), jnp.float32)

    @pl.when(jnp.logical_not(has_high))
    def _():
        ext[pl.ds((half + n_member) * tiles, half * tiles)] = jnp.zeros(
            (half * tiles, ROWS, 1, TILE), jnp.float32
        )

    for t in range(tiles):
        for c in range(3):
            row = place_row[c : c + 1, t * TILE : (t + 1) * TILE]
            tgt[t * 3 + c] = jnp.broadcast_to(row, (TILE, TILE)).T

    def one_pair(t, s, tile_id, first):
        keep = jnp.where(s < count_ref[t], SCALE, 0.0)

        def wide(c):
            return jnp.broadcast_to(ext[tile_id, c], (SUB, TILE))

        h = wide(2)
        src = (wide(0), wide(1), h, wide(3) * keep, wide(4) * keep, wide(5) * keep, h + h)
        for b in range(TILE // SUB):
            at = pl.ds(b * SUB, SUB)
            terms = pair_terms(tgt[t * 3, at], tgt[t * 3 + 1, at], tgt[t * 3 + 2, at], src)
            for c in range(3):
                if first:
                    acc[t * 3 + c, at] = terms[c]
                else:
                    acc[t * 3 + c, at] = acc[t * 3 + c, at] + terms[c]

    @pl.loop(0, tiles)
    def _(t):
        one_pair(t, 0, base + t, True)

    sized(block(0, n_member - 1), local_sem.at[0], data_sem.at[0]).wait_recv()

    @pl.when(has_low)
    def _():
        sized(block(0, half), local_sem.at[0], data_sem.at[1]).wait_recv()

    @pl.when(has_high)
    def _():
        sized(block(0, half), local_sem.at[0], data_sem.at[2]).wait_recv()

    zeros = jnp.zeros((VROWS - 3, TILE), jnp.float32)

    def vel_copy(t, step):
        part = vel.at[m, :, pl.ds(pl.multiple_of(t * TILE, TILE), TILE)]
        return move(part, part, local_sem.at[3], vel_sem.at[m], (r, other(step)))

    @pl.loop(0, tiles)
    def _(t):
        for s in range(1, pairs):
            one_pair(t, s, list_ref[t, s], False)
        rows = [jnp.sum(acc[t * 3 + c].T, axis=0, keepdims=True) for c in range(3)]
        at = pl.ds(pl.multiple_of(t * TILE, TILE), TILE)
        vel[m, :, at] = jnp.concatenate(rows + [zeros], axis=0)
        vel_out[:, at] = jnp.concatenate(rows, axis=0)
        for step in range(1, n_member):
            vel_copy(t, step).start()

    sized(ids.at[pl.ds(0, (n_member - 1) * tiles)], local_sem.at[2], data_sem.at[3]).wait_recv()
    width = hot.shape[1] // own_plates
    place = lax.broadcasted_iota(jnp.int32, (hot.shape[1], TILE), 0)

    @pl.loop(0, n_member)
    def _(e):
        for t in range(tiles):
            local = ids[e * tiles + t] - m * (own_plates * pb)
            row = jnp.full_like(local, -1)
            for k in range(own_plates):
                inside = jnp.logical_and(local >= k * pb, local < (k + 1) * pb)
                row = jnp.where(inside, local + k * (width - pb), row)
            hot[e, :, t * TILE : (t + 1) * TILE] = jnp.where(place == row, 1.0, 0.0).astype(jnp.bfloat16)

    def placed(e):
        return lax.dot_general(
            vel[e].astype(jnp.bfloat16),
            hot[e],
            (((1,), (1,)), ((), ())),
            preferred_element_type=jnp.float32,
        )

    body_all = placed(m)
    for step in range(1, n_member):
        e = other(step)
        sized(vel.at[e], local_sem.at[3], vel_sem.at[e]).wait_recv()
        body_all = body_all + placed(e)

    order = 3 * pb
    total = 2 * width
    bodies = []
    for k in range(own_plates):
        part = body_all[:, k * width : (k + 1) * width]
        part = jnp.concatenate([part, jnp.zeros((VROWS, total - width), jnp.float32)], axis=1)
        body = part[0:1]
        for c in range(1, 3):
            body = body + pltpu.roll(part, c * pb, 1)[c : c + 1]
        bodies.append(body[:, :order])
    body_out[...] = jnp.concatenate(bodies, axis=0).astype(jnp.bfloat16)

    sized(block(0, n_member - 1), local_sem.at[0], data_sem.at[0]).wait_send()
    sized(ids.at[pl.ds(0, (n_member - 1) * tiles)], local_sem.at[2], data_sem.at[3]).wait_send()
    sized(vel.at[pl.ds(0, n_member - 1)], local_sem.at[3], vel_sem.at[0]).wait_send()

    @pl.when(jnp.logical_or(to_high, to_low))
    def _():
        sized(block(0, n_member), local_sem.at[1], data_sem.at[1]).wait_send()


def finish(vel_ref, body_ref, vel_out, body_out):
    vel_out[...] = vel_ref[...]
    body_out[...] = body_ref[...]


def on_device(n_region, n_member, positions, forces, blob_platelet, blob_rank, owner, pair_list, pair_count, pre):
    blobs = positions.shape[1]
    tiles = blobs // TILE
    own_plates, order, _ = pre.shape
    pb = order // 3
    width = -(-pb // TILE) * TILE
    far = pl.BlockSpec(memory_space=pltpu.HBM)
    vector = pl.BlockSpec(memory_space=pltpu.VMEM)
    velocity, body_in = pl.pallas_call(
        functools.partial(kernel, n_region, n_member, pb, own_plates),
        out_shape=(
            pltpu.VMEM((3, blobs), jnp.float32),
            pltpu.VMEM((own_plates, order), jnp.bfloat16),
        ),
        in_specs=[far] * 7,
        out_specs=(vector, vector),
        scratch_shapes=[
            pltpu.VMEM((3, blobs), jnp.float32),
            pltpu.VMEM((3, blobs), jnp.float32),
            pltpu.VMEM((1, blobs), jnp.int32),
            pltpu.VMEM((1, blobs), jnp.int32),
            pltpu.SMEM(owner.shape, jnp.int32),
            pltpu.SMEM(pair_list.shape, jnp.int32),
            pltpu.SMEM(pair_count.shape, jnp.int32),
            pltpu.VMEM((2 * n_member * tiles, ROWS, 1, TILE), jnp.float32),
            pltpu.VMEM((n_member * tiles, 1, TILE), jnp.int32),
            pltpu.VMEM((3 * tiles, TILE, TILE), jnp.float32),
            pltpu.VMEM((3 * tiles, TILE, TILE), jnp.float32),
            pltpu.VMEM((n_member, VROWS, blobs), jnp.float32),
            pltpu.VMEM((n_member, own_plates * width, blobs), jnp.bfloat16),
            pltpu.SemaphoreType.DMA((7,)),
            pltpu.SemaphoreType.DMA((4,)),
            pltpu.SemaphoreType.DMA((n_member,)),
        ],
        compiler_params=pltpu.CompilerParams(collective_id=0, has_side_effects=True),
    )(
        positions,
        forces,
        blob_platelet,
        blob_rank,
        owner,
        pair_list,
        pair_count,
    )
    body_velocity = jnp.einsum("pab,pb->pa", pre, body_in, preferred_element_type=jnp.float32)
    return pl.pallas_call(
        finish,
        out_shape=(
            jax.ShapeDtypeStruct(velocity.shape, jnp.float32),
            jax.ShapeDtypeStruct(body_velocity.shape, jnp.float32),
        ),
        in_specs=[vector, vector],
        out_specs=(vector, vector),
        compiler_params=pltpu.CompilerParams(vmem_limit_bytes=1024 * 1024),
    )(velocity, body_velocity)


def solution(mesh):
    placed = (
        P(None, ("region", "member")),
        P(None, ("region", "member")),
        P(("region", "member")),
        P(("region", "member")),
        P("region"),
        P(("region", "member"), None),
        P(("region", "member")),
        P(("region", "member"), None, None),
    )
    return jax.shard_map(
        functools.partial(on_device, mesh.shape["region"], mesh.shape["member"]),
        mesh=mesh,
        in_specs=placed,
        out_specs=(P(None, ("region", "member")), P(("region", "member"), None)),
        check_vma=False,
    )
```

```python
import functools
import math

import jax
import jax.numpy as jnp
from jax import lax
from jax.experimental import pallas as pl
from jax.experimental.pallas import tpu as pltpu
from jax.sharding import PartitionSpec as P

TILE = 128
SUB = 8
VROWS = 4
ROWS = 8
PLANES = 4
DEPTH = 64
GATHER = 7
SCALE = 1.0 / (8.0 * math.pi)
MESH = pl.DeviceIdType.MESH


def split3(v):
    hi = v.astype(jnp.bfloat16).astype(jnp.float32)
    rest = v - hi
    mid = rest.astype(jnp.bfloat16).astype(jnp.float32)
    return hi, mid, rest - mid


def target_table(x):
    zero = jnp.zeros((1, TILE), jnp.float32)
    one = jnp.ones((1, TILE), jnp.float32)
    squares = jnp.sum(x * x, axis=0, keepdims=True)

    def plane(rows, tail=(), fixed=None):
        parts = list(zip(*[split3(v) for v in rows]))
        fixed = (zero, zero) if fixed is None else fixed
        blocks = []
        for k, part in enumerate((0, 0, 0, 1, 1, 2)):
            blocks += list(parts[part]) + (list(fixed) if k < 3 else [zero, zero])
        tail = list(split3(tail)) if len(tail) else [zero] * 3
        blocks += tail + [zero] * (DEPTH - len(blocks) - 3)
        blocks += [zero] * (TILE - DEPTH)
        return jnp.concatenate(blocks, axis=0).T[:, :DEPTH]

    x1, x2, x3 = x[0:1], x[1:2], x[2:3]
    none = [zero] * 3
    planes = [
        plane([-2.0 * x1, -2.0 * x2, -2.0 * x3] + none, squares + 1.0, (one, zero)),
        plane([-2.0 * x1, -2.0 * x2, 2.0 * x3] + none, squares, (one, zero)),
        plane(none + [x1, x2, x3], (), (zero, -one)),
        plane(none + [3.0 * x1, 3.0 * x2, -3.0 * x3], (), (zero, -3.0 * one)),
    ]
    rows = [p[b : b + SUB] for b in range(0, TILE, SUB) for p in planes]
    return jnp.concatenate(rows, axis=0).astype(jnp.bfloat16)


def source_table(rows, middle):
    row = lax.broadcasted_iota(jnp.int32, (SUB, TILE), 0)
    near = rows - middle
    squares = near * near
    products = near * pltpu.roll(near, SUB - 3, 0)

    def summed(v, at):
        v = v + pltpu.roll(v, SUB - 1, 0) + pltpu.roll(v, SUB - 2, 0)
        return pltpu.roll(v, at, 0)

    near = jnp.where(row == 6, summed(squares, 6), jnp.where(row == 7, summed(products, 7), near))
    hi, mid, lo = split3(near)
    ones = jnp.where(row < 3, 1.0, 0.0)
    spare = jnp.zeros((DEPTH - 7 * SUB, TILE), jnp.float32)
    return jnp.concatenate([hi, mid, lo, hi, mid, hi, ones, spare], axis=0).astype(jnp.bfloat16)


def gather_table(ext, count, table):
    section = lax.broadcasted_iota(jnp.int32, (3 * ROWS, TILE), 0) % ROWS
    spare = jnp.zeros((table.shape[1] - 3 * count - 3 * ROWS, TILE), jnp.float32)
    none = jnp.zeros((3 * ROWS, TILE), jnp.float32)
    turned = []
    for p, (c, factor) in enumerate(((0, -1.0), (1, -1.0), (2, -1.0), (2, 2.0), (3, 1.0), (4, 1.0), (5, 1.0))):
        parts = split3(ext[pl.ds(0, count), c, :] * factor)
        ones = jnp.where(section == p, 1.0, 0.0) if p < 3 else none
        turned.append(jnp.concatenate([*parts, ones, spare], axis=0).T)
    rows = [v[b : b + SUB] for b in range(0, TILE, SUB) for v in turned]
    table[...] = jnp.concatenate(rows, axis=0).astype(jnp.bfloat16)


def gathered_pairs(table, count, lists, parts, x3, pairs):
    x3 = jnp.broadcast_to(x3, (SUB, TILE))
    x3d = x3 + x3
    total = [jnp.zeros((SUB, TILE), jnp.float32)] * 3
    tile = lax.broadcasted_iota(jnp.int32, (count, TILE), 0).astype(jnp.float32)
    spare = jnp.zeros((table.shape[1] - 3 * count - 3 * ROWS, TILE), jnp.float32)
    for first in range(0, pairs, 2):
        columns = []
        for s in range(first, first + 2):
            chosen = jnp.where(lists[pairs : pairs + 1] > s, lists[s : s + 1], -1.0)
            hot = jnp.where(tile == chosen, 1.0, 0.0)
            columns.append(jnp.concatenate([hot, hot, hot, *parts, spare], axis=0))
        columns = jnp.concatenate(columns, axis=1).astype(jnp.bfloat16)
        planes = jnp.dot(table[...], columns, preferred_element_type=jnp.float32)
        for side in range(2):
            for b in range(TILE // SUB):
                d1, d2, d3, h2, f1, f2, f3 = [
                    planes[(b * GATHER + p) * SUB :][:SUB, side * TILE : (side + 1) * TILE] for p in range(GATHER)
                ]
                dd = d1 * d1 + d2 * d2 + d3 * d3
                c = h2 * x3
                w = lax.rsqrt(dd + 1.0)
                p = lax.rsqrt(dd + (c + c))
                w3 = w * w * w
                p2 = p * p
                p3 = p2 * p
                full = d1 * f1 + d2 * f2 + d3 * f3
                mirror = full - x3d * f3
                cp3 = c * p3
                alpha = (w + w3) - (p + cp3)
                gamma = 3.0 * (cp3 * p2) * mirror
                both = full * (w3 - p3) + gamma
                total[0] = total[0] + (f1 * alpha + d1 * both)
                total[1] = total[1] + (f2 * alpha + d2 * both)
                total[2] = total[2] + (f3 * alpha + d3 * both + h2 * gamma)
    return [jnp.sum(v, axis=0, keepdims=True) for v in total]


def kernel(
    n_region,
    n_member,
    pb,
    own_plates,
    pos_hbm,
    force_hbm,
    plate_hbm,
    rank_hbm,
    owner_hbm,
    list_hbm,
    count_hbm,
    vel_out,
    body_out,
    pos,
    force,
    plate,
    rank,
    owner_ref,
    list_ref,
    count_ref,
    ext,
    ids,
    sources,
    targets,
    tgt,
    acc,
    table,
    vel,
    hot,
    local_sem,
    data_sem,
    vel_sem,
):
    r = lax.axis_index("region")
    m = lax.axis_index("member")
    half = n_member // 2
    tiles = pos.shape[1] // TILE
    blobs = pos.shape[1]
    plates = owner_ref.shape[0]
    pairs = list_ref.shape[1]
    has_low = r > 0
    has_high = r < n_region - 1
    to_high = jnp.logical_and(m >= half, has_high)
    to_low = jnp.logical_and(m < half, has_low)
    base = (half + m) * tiles

    far = n_member - 1 - m
    lower = jnp.where(m < half, m, far)

    def peer(j):
        mate = lax.rem(lower + 1 + j // 2, half)
        return jnp.where(j % 2 == 0, mate, n_member - 1 - mate)

    peers = [peer(j) for j in range(n_member - 2)]
    others = peers + [far]

    barrier = pltpu.get_barrier_semaphore()
    for e in others:
        pl.semaphore_signal(barrier, inc=1, device_id=(r, e), device_id_type=MESH)

    loads = [
        pltpu.make_async_copy(a, b, local_sem.at[i])
        for i, (a, b) in enumerate(
            ((pos_hbm, pos), (force_hbm, force), (plate_hbm, plate.at[0]), (rank_hbm, rank.at[0]),
             (owner_hbm, owner_ref), (list_hbm, list_ref), (count_hbm, count_ref))
        )
    ]
    for load in loads[:3]:
        load.start()

    @pl.when(has_low)
    def _():
        for k in range(half):
            pl.semaphore_signal(barrier, inc=1, device_id=(r - 1, half + k), device_id_type=MESH)

    @pl.when(has_high)
    def _():
        for k in range(half):
            pl.semaphore_signal(barrier, inc=1, device_id=(r + 1, k), device_id_type=MESH)

    for load in loads[3:]:
        load.start()

    for load in loads[:3]:
        load.wait()

    live = plate[...] < plates
    place_row = pos[...]
    push_row = force[...] * jnp.where(live, SCALE, 0.0)
    packed = jnp.concatenate([place_row, push_row, jnp.zeros((ROWS - 6, blobs), jnp.float32)], axis=0)
    for t in range(tiles):
        ext[base + t] = packed[:, t * TILE : (t + 1) * TILE]

    def block(e, count=1):
        return ext.at[pl.ds(e * tiles, count * tiles)]

    def move(src, dst, send, recv, to):
        return pltpu.make_async_remote_copy(
            src_ref=src, dst_ref=dst, send_sem=send, recv_sem=recv, device_id=to, device_id_type=MESH
        )

    def near_copy(e):
        here = block(half + m)
        return move(here, here, local_sem.at[0], data_sem.at[0], (r, e))

    def rim_copy(k, shift, e, sem):
        return move(block(half + m), block(e), local_sem.at[1], data_sem.at[sem], (r + shift, lax.rem(m + k, n_member)))

    def sized(ref, send, recv):
        return move(ref, ref, send, recv, (r, far))

    rim_sends = jnp.where(jnp.logical_or(to_high, to_low), n_member, 0)
    pl.semaphore_wait(barrier, n_member - 1 + rim_sends)

    for e in others:
        near_copy(e).start()

    @pl.when(to_high)
    def _():
        for k in range(n_member):
            rim_copy(k, 1, m - half, 1).start()

    @pl.when(to_low)
    def _():
        for k in range(n_member):
            rim_copy(k, -1, half + n_member + m, 2).start()

    for load in loads[3:]:
        load.wait()

    plate_row = plate[...]
    slot_of = jnp.zeros_like(plate_row)
    for k in range(plates):
        slot_of = jnp.where(plate_row == k, owner_ref[k], slot_of)
    body_at = jnp.where(live, slot_of * pb + rank[...], plates * pb)
    lane = lax.broadcasted_iota(jnp.int32, (1, TILE), 1)
    for t in range(tiles):
        info = jnp.where(lane == pairs, count_ref[t], 0)
        for s in range(pairs):
            info = jnp.where(lane == s, list_ref[t, s], info)
        ids[m * tiles + t] = jnp.concatenate([body_at[:, t * TILE : (t + 1) * TILE], info], axis=0)

    def ids_copy(e):
        here = ids.at[pl.ds(m * tiles, tiles)]
        return move(here, here, local_sem.at[2], data_sem.at[3], (r, e))

    for e in others:
        ids_copy(e).start()

    @pl.when(jnp.logical_not(has_low))
    def _():
        ext[pl.ds(0, half * tiles)] = jnp.zeros((half * tiles, ROWS, TILE), jnp.float32)

    @pl.when(jnp.logical_not(has_high))
    def _():
        ext[pl.ds((half + n_member) * tiles, half * tiles)] = jnp.zeros(
            (half * tiles, ROWS, TILE), jnp.float32
        )

    across = lax.broadcasted_iota(jnp.int32, (ROWS, TILE), 0) < 2
    middle = jnp.where(across, jnp.broadcast_to(packed[:, :1], (ROWS, TILE)), 0.0)
    last = ext.shape[0] - 1
    ext[last] = jnp.zeros((ROWS, TILE), jnp.float32)
    sources[last] = source_table(jnp.zeros((ROWS, TILE), jnp.float32), middle)

    def tabulate(first, count):
        @pl.loop(0, count)
        def _(i):
            for t in range(tiles):
                at = first + i * tiles + t
                sources[at] = source_table(ext[at], middle)

    tabulate(base, 1)
    for t in range(tiles):
        own = place_row[:, t * TILE : (t + 1) * TILE]
        for c in range(3):
            tgt[t * 3 + c] = jnp.broadcast_to(own[c : c + 1], (TILE, TILE)).T
        targets[t] = target_table(own - middle[:3])

    def some_pairs(t, tile_ids, first):
        columns = jnp.concatenate([sources[e] for e in tile_ids], axis=1)
        planes = jnp.dot(targets[t], columns, preferred_element_type=jnp.float32)
        for side, e in enumerate(tile_ids):
            rows = ext[e]
            y1, y2, h, f1, f2, f3 = [jnp.broadcast_to(rows[c : c + 1], (SUB, TILE)) for c in range(6)]
            h2 = h + h
            for b in range(TILE // SUB):
                at = pl.ds(b * SUB, SUB)
                near, image, full, mirror = [
                    planes[(b * PLANES + p) * SUB :][:SUB, side * TILE : (side + 1) * TILE]
                    for p in range(PLANES)
                ]
                d1 = tgt[t * 3, at] - y1
                d2 = tgt[t * 3 + 1, at] - y2
                x3 = tgt[t * 3 + 2, at]
                d3 = x3 - h
                w = lax.rsqrt(near)
                p = lax.rsqrt(image)
                w3 = w * w * w
                p2 = p * p
                p3 = p2 * p
                cp3 = (h2 * x3) * p3
                alpha = (w + w3) - (p + cp3)
                gamma = cp3 * p2 * mirror
                both = full * (w3 - p3) + gamma
                terms = (f1 * alpha + d1 * both, f2 * alpha + d2 * both, f3 * alpha + d3 * both + h2 * gamma)
                for k in range(3):
                    if first:
                        acc[t * 3 + k, at] = terms[k]
                    else:
                        acc[t * 3 + k, at] = acc[t * 3 + k, at] + terms[k]

    @pl.loop(0, tiles)
    def _(t):
        some_pairs(t, [base + t], True)

    sized(block(0, n_member - 1), local_sem.at[0], data_sem.at[0]).wait_recv()

    for e in others:
        tabulate((half + e) * tiles, 1)

    @pl.when(has_low)
    def _():
        sized(block(0, half), local_sem.at[0], data_sem.at[1]).wait_recv()

    @pl.when(has_high)
    def _():
        sized(block(0, half), local_sem.at[0], data_sem.at[2]).wait_recv()

    tabulate(0, half)
    tabulate((half + n_member) * tiles, half)
    zeros = jnp.zeros((VROWS - 3, TILE), jnp.float32)

    def vel_copy(e):
        return move(vel.at[m], vel.at[m], local_sem.at[3], vel_sem.at[m], (r, e))

    blocks = []
    for t in range(tiles):
        for s in range(1, pairs, 2):
            chosen = [jnp.where(k < count_ref[t], list_ref[t, k], last) for k in range(s, min(s + 2, pairs))]
            some_pairs(t, chosen, False)
        blocks.append([jnp.sum(acc[t * 3 + c].T, axis=0, keepdims=True) for c in range(3)] + [zeros])
    rows = jnp.concatenate([jnp.concatenate(block, axis=0) for block in blocks], axis=1)
    vel[m] = rows
    for e in peers:
        vel_copy(e).start()
    vel_out[...] = rows[:3]

    count = 2 * n_member * tiles
    gather_table(ext, count, table)

    sized(ids.at[pl.ds(0, (n_member - 1) * tiles)], local_sem.at[2], data_sem.at[3]).wait_recv()
    first_id = m * (own_plates * pb)
    room = own_plates * pb
    far_ids = [ids[far * tiles + t] for t in range(tiles)]
    local = jnp.concatenate([v[:1] for v in far_ids], axis=0) - first_id
    mine = jnp.logical_and(local >= 0, local < room)
    counted = jnp.concatenate(
        [mine.astype(jnp.float32), jnp.zeros((2 * SUB - tiles, TILE), jnp.float32)], axis=0
    ).astype(jnp.bfloat16)
    up_to = lax.broadcasted_iota(jnp.int32, (TILE, TILE), 0) <= lax.broadcasted_iota(jnp.int32, (TILE, TILE), 1)
    order_in = jnp.dot(
        counted, jnp.where(up_to, 1.0, 0.0).astype(jnp.bfloat16), preferred_element_type=jnp.float32
    )
    seat = lax.broadcasted_iota(jnp.int32, (TILE, TILE), 0).astype(jnp.float32)
    row = lax.broadcasted_iota(jnp.int32, (ROWS, TILE), 0)
    before = jnp.full((1, 1), -1.0, jnp.float32)
    chosen, columns = [], []
    for t in range(tiles):
        at = jnp.where(mine[t : t + 1], order_in[t : t + 1] + before, -1.0)
        before = before + order_in[t : t + 1, TILE - 1 :]
        chosen.append(jnp.where(seat == at, 1.0, 0.0))
        id_hi, id_lo, _ = split3(local[t : t + 1].astype(jnp.float32))
        extra = jnp.where(row == 0, t + 1.0, jnp.where(row == 1, id_hi, jnp.where(row == 2, id_lo, 0.0)))
        columns.append(jnp.concatenate([*split3(ext[(half + far) * tiles + t]), extra], axis=0))
    picked = lax.dot_general(
        jnp.concatenate(columns, axis=1).astype(jnp.bfloat16),
        jnp.concatenate(chosen, axis=1).astype(jnp.bfloat16),
        (((1,), (1,)), ((), ())),
        preferred_element_type=jnp.float32,
    )
    label = picked[3 * ROWS : 3 * ROWS + 1]
    far_id = picked[3 * ROWS + 1 : 3 * ROWS + 2] + picked[3 * ROWS + 2 : 3 * ROWS + 3]
    info = jnp.concatenate([v[1:] for v in far_ids], axis=0).astype(jnp.float32)
    info = jnp.concatenate([info, jnp.zeros((TILE - tiles, TILE), jnp.float32)], axis=0).T
    of_tile = lax.broadcasted_iota(jnp.int32, (2 * SUB, TILE), 0).astype(jnp.float32) + 1.0
    lists = jnp.dot(
        info[: 2 * SUB, : 2 * SUB].astype(jnp.bfloat16),
        jnp.where(of_tile == label, 1.0, 0.0).astype(jnp.bfloat16),
        preferred_element_type=jnp.float32,
    )
    unused = jnp.logical_and(row == 2, label == 0.0)
    parts = [jnp.where(unused, 1.0, picked[:ROWS]), picked[ROWS : 2 * ROWS], picked[2 * ROWS : 3 * ROWS]]
    x3 = (parts[0] + parts[1] + parts[2])[2:3]

    far_vel = jnp.concatenate(gathered_pairs(table, count, lists, parts, x3, pairs) + [zeros], axis=0)

    width = hot.shape[1] // own_plates
    place = lax.broadcasted_iota(jnp.int32, (hot.shape[1], TILE), 0)
    place_f = place.astype(jnp.float32)

    @pl.loop(0, n_member - 1)
    def _(j):
        e = jnp.where(j == 0, m, peer(jnp.maximum(j - 1, 0)))
        for t in range(tiles):
            local = ids[e * tiles + t][:1] - first_id
            row = jnp.full_like(local, -1)
            for k in range(own_plates):
                inside = jnp.logical_and(local >= k * pb, local < (k + 1) * pb)
                row = jnp.where(inside, local + k * (width - pb), row)
            hot[j, :, t * TILE : (t + 1) * TILE] = jnp.where(place == row, 1.0, 0.0).astype(jnp.bfloat16)

    def placed(e, hot_at):
        return lax.dot_general(
            vel[e].astype(jnp.bfloat16), hot_at, (((1,), (1,)), ((), ())), preferred_element_type=jnp.float32
        )

    far_row = jnp.full((1, TILE), -1.0, jnp.float32)
    for k in range(own_plates):
        inside = jnp.logical_and(far_id >= k * pb, far_id < (k + 1) * pb)
        far_row = jnp.where(inside, far_id + float(k * (width - pb)), far_row)
    far_row = jnp.where(label == 0.0, -1.0, far_row)
    far_hot = jnp.where(place_f == far_row, 1.0, 0.0).astype(jnp.bfloat16)
    far_vel = jnp.where(label == 0.0, 0.0, far_vel)

    body_all = placed(m, hot[0]) + lax.dot_general(
        far_vel.astype(jnp.bfloat16), far_hot, (((1,), (1,)), ((), ())), preferred_element_type=jnp.float32
    )
    for j, e in enumerate(peers):
        sized(vel.at[e], local_sem.at[3], vel_sem.at[e]).wait_recv()
        body_all = body_all + placed(e, hot[j + 1])

    order = 3 * pb
    total = 2 * width
    bodies = []
    for k in range(own_plates):
        part = body_all[:, k * width : (k + 1) * width]
        part = jnp.concatenate([part, jnp.zeros((VROWS, total - width), jnp.float32)], axis=1)
        body = part[0:1]
        for c in range(1, 3):
            body = body + pltpu.roll(part, c * pb, 1)[c : c + 1]
        bodies.append(body[:, :order])
    body_out[...] = jnp.concatenate(bodies, axis=0).astype(jnp.bfloat16)

    sized(block(0, n_member - 1), local_sem.at[0], data_sem.at[0]).wait_send()
    sized(ids.at[pl.ds(0, (n_member - 1) * tiles)], local_sem.at[2], data_sem.at[3]).wait_send()
    sized(vel.at[pl.ds(0, n_member - 2)], local_sem.at[3], vel_sem.at[0]).wait_send()

    @pl.when(jnp.logical_or(to_high, to_low))
    def _():
        sized(block(0, n_member), local_sem.at[1], data_sem.at[1]).wait_send()


def finish(vel_ref, body_ref, vel_out, body_out):
    vel_out[...] = vel_ref[...]
    body_out[...] = body_ref[...]


def on_device(n_region, n_member, positions, forces, blob_platelet, blob_rank, owner, pair_list, pair_count, pre):
    blobs = positions.shape[1]
    tiles = blobs // TILE
    own_plates, order, _ = pre.shape
    pb = order // 3
    width = -(-pb // TILE) * TILE
    depth = -(-3 * (2 * n_member * tiles + ROWS) // TILE) * TILE
    far = pl.BlockSpec(memory_space=pltpu.HBM)
    vector = pl.BlockSpec(memory_space=pltpu.VMEM)
    velocity, body_in = pl.pallas_call(
        functools.partial(kernel, n_region, n_member, pb, own_plates),
        out_shape=(
            pltpu.VMEM((3, blobs), jnp.float32),
            pltpu.VMEM((own_plates, order), jnp.bfloat16),
        ),
        in_specs=[far] * 7,
        out_specs=(vector, vector),
        scratch_shapes=[
            pltpu.VMEM((3, blobs), jnp.float32),
            pltpu.VMEM((3, blobs), jnp.float32),
            pltpu.VMEM((1, blobs), jnp.int32),
            pltpu.VMEM((1, blobs), jnp.int32),
            pltpu.SMEM(owner.shape, jnp.int32),
            pltpu.SMEM(pair_list.shape, jnp.int32),
            pltpu.SMEM(pair_count.shape, jnp.int32),
            pltpu.VMEM((2 * n_member * tiles + 1, ROWS, TILE), jnp.float32),
            pltpu.VMEM((n_member * tiles, 2, TILE), jnp.int32),
            pltpu.VMEM((2 * n_member * tiles + 1, DEPTH, TILE), jnp.bfloat16),
            pltpu.VMEM((tiles, PLANES * TILE, DEPTH), jnp.bfloat16),
            pltpu.VMEM((3 * tiles, TILE, TILE), jnp.float32),
            pltpu.VMEM((3 * tiles, TILE, TILE), jnp.float32),
            pltpu.VMEM((GATHER * TILE, depth), jnp.bfloat16),
            pltpu.VMEM((n_member, VROWS, blobs), jnp.float32),
            pltpu.VMEM((n_member - 1, own_plates * width, blobs), jnp.bfloat16),
            pltpu.SemaphoreType.DMA((7,)),
            pltpu.SemaphoreType.DMA((4,)),
            pltpu.SemaphoreType.DMA((n_member,)),
        ],
        compiler_params=pltpu.CompilerParams(collective_id=0, has_side_effects=True),
    )(
        positions,
        forces,
        blob_platelet,
        blob_rank,
        owner,
        pair_list,
        pair_count,
    )
    body_velocity = jnp.einsum("pab,pb->pa", pre, body_in, preferred_element_type=jnp.float32)
    return pl.pallas_call(
        finish,
        out_shape=(
            jax.ShapeDtypeStruct(velocity.shape, jnp.float32),
            jax.ShapeDtypeStruct(body_velocity.shape, jnp.float32),
        ),
        in_specs=[vector, vector],
        out_specs=(vector, vector),
        compiler_params=pltpu.CompilerParams(vmem_limit_bytes=1024 * 1024),
    )(velocity, body_velocity)


def solution(mesh):
    placed = (
        P(None, ("region", "member")),
        P(None, ("region", "member")),
        P(("region", "member")),
        P(("region", "member")),
        P("region"),
        P(("region", "member"), None),
        P(("region", "member")),
        P(("region", "member"), None, None),
    )
    return jax.shard_map(
        functools.partial(on_device, mesh.shape["region"], mesh.shape["member"]),
        mesh=mesh,
        in_specs=placed,
        out_specs=(P(None, ("region", "member")), P(("region", "member"), None)),
        check_vma=False,
    )
```

```python
import functools
import math

import jax
import jax.numpy as jnp
from jax import lax
from jax.experimental import pallas as pl
from jax.experimental.pallas import tpu as pltpu
from jax.sharding import PartitionSpec as P

TILE = 128
SUB = 8
VROWS = 4
ROWS = 8
PLANES = 4
DEPTH = 64
GATHER = 7
SCALE = 1.0 / (8.0 * math.pi)
MESH = pl.DeviceIdType.MESH


def split3(v):
    hi = v.astype(jnp.bfloat16).astype(jnp.float32)
    rest = v - hi
    mid = rest.astype(jnp.bfloat16).astype(jnp.float32)
    return hi, mid, rest - mid


def target_table(x):
    zero = jnp.zeros((1, TILE), jnp.float32)
    one = jnp.ones((1, TILE), jnp.float32)
    squares = jnp.sum(x * x, axis=0, keepdims=True)

    def plane(rows, tail=(), fixed=None):
        parts = list(zip(*[split3(v) for v in rows]))
        fixed = (zero, zero) if fixed is None else fixed
        blocks = []
        for k, part in enumerate((0, 0, 0, 1, 1, 2)):
            blocks += list(parts[part]) + (list(fixed) if k < 3 else [zero, zero])
        tail = list(split3(tail)) if len(tail) else [zero] * 3
        blocks += tail + [zero] * (DEPTH - len(blocks) - 3)
        blocks += [zero] * (TILE - DEPTH)
        return jnp.concatenate(blocks, axis=0).T[:, :DEPTH]

    x1, x2, x3 = x[0:1], x[1:2], x[2:3]
    none = [zero] * 3
    planes = [
        plane([-2.0 * x1, -2.0 * x2, -2.0 * x3] + none, squares + 1.0, (one, zero)),
        plane([-2.0 * x1, -2.0 * x2, 2.0 * x3] + none, squares, (one, zero)),
        plane(none + [x1, x2, x3], (), (zero, -one)),
        plane(none + [3.0 * x1, 3.0 * x2, -3.0 * x3], (), (zero, -3.0 * one)),
    ]
    rows = [p[b : b + SUB] for b in range(0, TILE, SUB) for p in planes]
    return jnp.concatenate(rows, axis=0).astype(jnp.bfloat16)


def source_table(rows, middle):
    row = lax.broadcasted_iota(jnp.int32, (SUB, TILE), 0)
    near = rows - middle
    squares = near * near
    products = near * pltpu.roll(near, SUB - 3, 0)

    def summed(v, at):
        v = v + pltpu.roll(v, SUB - 1, 0) + pltpu.roll(v, SUB - 2, 0)
        return pltpu.roll(v, at, 0)

    near = jnp.where(row == 6, summed(squares, 6), jnp.where(row == 7, summed(products, 7), near))
    hi, mid, lo = split3(near)
    ones = jnp.where(row < 3, 1.0, 0.0)
    spare = jnp.zeros((DEPTH - 7 * SUB, TILE), jnp.float32)
    return jnp.concatenate([hi, mid, lo, hi, mid, hi, ones, spare], axis=0).astype(jnp.bfloat16)


def gather_table(ext, count, table):
    section = lax.broadcasted_iota(jnp.int32, (3 * ROWS, TILE), 0) % ROWS
    spare = jnp.zeros((table.shape[1] - 3 * count - 3 * ROWS, TILE), jnp.float32)
    none = jnp.zeros((3 * ROWS, TILE), jnp.float32)
    turned = []
    for p, (c, factor) in enumerate(((0, -1.0), (1, -1.0), (2, -1.0), (2, 2.0), (3, 1.0), (4, 1.0), (5, 1.0))):
        parts = split3(ext[pl.ds(0, count), c, :] * factor)
        ones = jnp.where(section == p, 1.0, 0.0) if p < 3 else none
        turned.append(jnp.concatenate([*parts, ones, spare], axis=0).T)
    rows = [v[b : b + SUB] for b in range(0, TILE, SUB) for v in turned]
    table[...] = jnp.concatenate(rows, axis=0).astype(jnp.bfloat16)


def gathered_pairs(table, count, lists, parts, x3, pairs):
    x3 = jnp.broadcast_to(x3, (SUB, TILE))
    x3d = x3 + x3
    total = [jnp.zeros((SUB, TILE), jnp.float32)] * 3
    tile = lax.broadcasted_iota(jnp.int32, (count, TILE), 0).astype(jnp.float32)
    spare = jnp.zeros((table.shape[1] - 3 * count - 3 * ROWS, TILE), jnp.float32)
    for first in range(0, pairs, 2):
        columns = []
        for s in range(first, first + 2):
            chosen = jnp.where(lists[pairs : pairs + 1] > s, lists[s : s + 1], -1.0)
            hot = jnp.where(tile == chosen, 1.0, 0.0)
            columns.append(jnp.concatenate([hot, hot, hot, *parts, spare], axis=0))
        columns = jnp.concatenate(columns, axis=1).astype(jnp.bfloat16)
        planes = jnp.dot(table[...], columns, preferred_element_type=jnp.float32)
        for side in range(2):
            for b in range(TILE // SUB):
                d1, d2, d3, h2, f1, f2, f3 = [
                    planes[(b * GATHER + p) * SUB :][:SUB, side * TILE : (side + 1) * TILE] for p in range(GATHER)
                ]
                dd = d1 * d1 + d2 * d2 + d3 * d3
                c = h2 * x3
                w = lax.rsqrt(dd + 1.0)
                p = lax.rsqrt(dd + (c + c))
                w3 = w * w * w
                p2 = p * p
                p3 = p2 * p
                full = d1 * f1 + d2 * f2 + d3 * f3
                mirror = full - x3d * f3
                cp3 = c * p3
                alpha = (w + w3) - (p + cp3)
                gamma = 3.0 * (cp3 * p2) * mirror
                both = full * (w3 - p3) + gamma
                total[0] = total[0] + (f1 * alpha + d1 * both)
                total[1] = total[1] + (f2 * alpha + d2 * both)
                total[2] = total[2] + (f3 * alpha + d3 * both + h2 * gamma)
    return [jnp.sum(v, axis=0, keepdims=True) for v in total]


def kernel(
    n_region,
    n_member,
    pb,
    own_plates,
    pos_hbm,
    force_hbm,
    plate_hbm,
    rank_hbm,
    owner_hbm,
    list_hbm,
    count_hbm,
    vel_out,
    body_out,
    pos,
    force,
    plate,
    rank,
    owner_ref,
    list_ref,
    count_ref,
    ext,
    sources,
    targets,
    tgt,
    acc,
    table,
    vel,
    hot,
    local_sem,
    data_sem,
    vel_sem,
):
    r = lax.axis_index("region")
    m = lax.axis_index("member")
    half = n_member // 2
    tiles = pos.shape[1] // TILE
    blobs = pos.shape[1]
    plates = owner_ref.shape[0]
    pairs = list_ref.shape[1]
    has_low = r > 0
    has_high = r < n_region - 1
    to_high = jnp.logical_and(m >= half, has_high)
    to_low = jnp.logical_and(m < half, has_low)
    base = (half + m) * tiles

    far = n_member - 1 - m
    lower = jnp.where(m < half, m, far)

    def peer(j):
        mate = lax.rem(lower + 1 + j // 2, half)
        return jnp.where(j % 2 == 0, mate, n_member - 1 - mate)

    peers = [peer(j) for j in range(n_member - 2)]
    others = [far] + peers

    barrier = pltpu.get_barrier_semaphore()
    for e in others:
        pl.semaphore_signal(barrier, inc=1, device_id=(r, e), device_id_type=MESH)

    loads = [
        pltpu.make_async_copy(a, b, local_sem.at[i])
        for i, (a, b) in enumerate(
            ((pos_hbm, pos), (force_hbm, force), (plate_hbm, plate.at[0]), (rank_hbm, rank.at[0]),
             (owner_hbm, owner_ref), (list_hbm, list_ref), (count_hbm, count_ref))
        )
    ]
    for load in loads[:3]:
        load.start()

    @pl.when(has_low)
    def _():
        for k in range(half):
            pl.semaphore_signal(barrier, inc=1, device_id=(r - 1, half + k), device_id_type=MESH)

    @pl.when(has_high)
    def _():
        for k in range(half):
            pl.semaphore_signal(barrier, inc=1, device_id=(r + 1, k), device_id_type=MESH)

    for load in loads[3:]:
        load.start()

    for load in loads:
        load.wait()

    live = plate[...] < plates
    place_row = pos[...]
    push_row = force[...] * jnp.where(live, SCALE, 0.0)
    plate_row = plate[...]
    slot_of = jnp.zeros_like(plate_row)
    for k in range(plates):
        slot_of = jnp.where(plate_row == k, owner_ref[k], slot_of)
    body_at = jnp.where(live, slot_of * pb + rank[...], plates * pb).astype(jnp.float32)
    lane = lax.broadcasted_iota(jnp.int32, (1, TILE), 1)
    for t in range(tiles):
        span = slice(t * TILE, (t + 1) * TILE)
        info = jnp.where(lane == pairs, count_ref[t], 0)
        for s in range(pairs):
            info = jnp.where(lane == s, list_ref[t, s], info)
        ext[base + t] = jnp.concatenate(
            [place_row[:, span], push_row[:, span], body_at[:, span], info.astype(jnp.float32)], axis=0
        )

    def block(e, count=1):
        return ext.at[pl.ds(e * tiles, count * tiles)]

    def move(src, dst, send, recv, to):
        return pltpu.make_async_remote_copy(
            src_ref=src, dst_ref=dst, send_sem=send, recv_sem=recv, device_id=to, device_id_type=MESH
        )

    def near_copy(e):
        here = block(half + m)
        return move(here, here, local_sem.at[0], data_sem.at[0], (r, e))

    def rim_copy(k, shift, e, sem):
        return move(block(half + m), block(e), local_sem.at[1], data_sem.at[sem], (r + shift, lax.rem(m + k, n_member)))

    def sized(ref, send, recv):
        return move(ref, ref, send, recv, (r, far))

    rim_sends = jnp.where(jnp.logical_or(to_high, to_low), n_member, 0)
    pl.semaphore_wait(barrier, n_member - 1 + rim_sends)

    for e in others:
        near_copy(e).start()

    @pl.when(to_high)
    def _():
        for k in range(n_member):
            rim_copy(k, 1, m - half, 1).start()

    @pl.when(to_low)
    def _():
        for k in range(n_member):
            rim_copy(k, -1, half + n_member + m, 2).start()

    @pl.when(jnp.logical_not(has_low))
    def _():
        ext[pl.ds(0, half * tiles)] = jnp.zeros((half * tiles, ROWS, TILE), jnp.float32)

    @pl.when(jnp.logical_not(has_high))
    def _():
        ext[pl.ds((half + n_member) * tiles, half * tiles)] = jnp.zeros(
            (half * tiles, ROWS, TILE), jnp.float32
        )

    across = lax.broadcasted_iota(jnp.int32, (ROWS, TILE), 0) < 2
    middle = jnp.where(across, jnp.broadcast_to(ext[base][:, :1], (ROWS, TILE)), 0.0)
    last = ext.shape[0] - 1
    ext[last] = jnp.zeros((ROWS, TILE), jnp.float32)
    sources[last] = source_table(jnp.zeros((ROWS, TILE), jnp.float32), middle)

    def tabulate(first, count):
        @pl.loop(0, count)
        def _(i):
            for t in range(tiles):
                at = first + i * tiles + t
                sources[at] = source_table(ext[at], middle)

    tabulate(base, 1)
    for t in range(tiles):
        own = place_row[:, t * TILE : (t + 1) * TILE]
        for c in range(3):
            tgt[t * 3 + c] = jnp.broadcast_to(own[c : c + 1], (TILE, TILE)).T
        targets[t] = target_table(own - middle[:3])

    def some_pairs(t, tile_ids, first):
        columns = jnp.concatenate([sources[e] for e in tile_ids], axis=1)
        planes = jnp.dot(targets[t], columns, preferred_element_type=jnp.float32)
        for side, e in enumerate(tile_ids):
            rows = ext[e]
            y1, y2, h, f1, f2, f3 = [jnp.broadcast_to(rows[c : c + 1], (SUB, TILE)) for c in range(6)]
            h2 = h + h
            for b in range(TILE // SUB):
                at = pl.ds(b * SUB, SUB)
                near, image, full, mirror = [
                    planes[(b * PLANES + p) * SUB :][:SUB, side * TILE : (side + 1) * TILE]
                    for p in range(PLANES)
                ]
                d1 = tgt[t * 3, at] - y1
                d2 = tgt[t * 3 + 1, at] - y2
                x3 = tgt[t * 3 + 2, at]
                d3 = x3 - h
                w = lax.rsqrt(near)
                p = lax.rsqrt(image)
                w3 = w * w * w
                p2 = p * p
                p3 = p2 * p
                cp3 = (h2 * x3) * p3
                alpha = (w + w3) - (p + cp3)
                gamma = cp3 * p2 * mirror
                both = full * (w3 - p3) + gamma
                terms = (f1 * alpha + d1 * both, f2 * alpha + d2 * both, f3 * alpha + d3 * both + h2 * gamma)
                for k in range(3):
                    if first:
                        acc[t * 3 + k, at] = terms[k]
                    else:
                        acc[t * 3 + k, at] = acc[t * 3 + k, at] + terms[k]

    @pl.loop(0, tiles)
    def _(t):
        some_pairs(t, [base + t], True)

    sized(block(0, n_member - 1), local_sem.at[0], data_sem.at[0]).wait_recv()

    for e in others:
        tabulate((half + e) * tiles, 1)

    @pl.when(has_low)
    def _():
        sized(block(0, half), local_sem.at[0], data_sem.at[1]).wait_recv()

    @pl.when(has_high)
    def _():
        sized(block(0, half), local_sem.at[0], data_sem.at[2]).wait_recv()

    tabulate(0, half)
    tabulate((half + n_member) * tiles, half)
    zeros = jnp.zeros((VROWS - 3, TILE), jnp.float32)

    def vel_copy(e):
        return move(vel.at[m], vel.at[m], local_sem.at[3], vel_sem.at[m], (r, e))

    blocks = []
    for t in range(tiles):
        for s in range(1, pairs, 2):
            chosen = [jnp.where(k < count_ref[t], list_ref[t, k], last) for k in range(s, min(s + 2, pairs))]
            some_pairs(t, chosen, False)
        blocks.append([jnp.sum(acc[t * 3 + c].T, axis=0, keepdims=True) for c in range(3)] + [zeros])
    rows = jnp.concatenate([jnp.concatenate(block, axis=0) for block in blocks], axis=1)
    vel[m] = rows
    for e in peers:
        vel_copy(e).start()
    vel_out[...] = rows[:3]

    count = 2 * n_member * tiles
    gather_table(ext, count, table)

    first_id = (m * (own_plates * pb)).astype(jnp.float32)
    room = own_plates * pb
    far_tiles = [ext[(half + far) * tiles + t] for t in range(tiles)]
    local = jnp.concatenate([v[6:7] for v in far_tiles], axis=0) - first_id
    mine = jnp.logical_and(local >= 0.0, local < float(room))
    counted = jnp.concatenate(
        [mine.astype(jnp.float32), jnp.zeros((2 * SUB - tiles, TILE), jnp.float32)], axis=0
    ).astype(jnp.bfloat16)
    up_to = lax.broadcasted_iota(jnp.int32, (TILE, TILE), 0) <= lax.broadcasted_iota(jnp.int32, (TILE, TILE), 1)
    order_in = jnp.dot(
        counted, jnp.where(up_to, 1.0, 0.0).astype(jnp.bfloat16), preferred_element_type=jnp.float32
    )
    seat = lax.broadcasted_iota(jnp.int32, (TILE, TILE), 0).astype(jnp.float32)
    row = lax.broadcasted_iota(jnp.int32, (ROWS, TILE), 0)
    before = jnp.full((1, 1), -1.0, jnp.float32)
    chosen, columns = [], []
    for t in range(tiles):
        at = jnp.where(mine[t : t + 1], order_in[t : t + 1] + before, -1.0)
        before = before + order_in[t : t + 1, TILE - 1 :]
        chosen.append(jnp.where(seat == at, 1.0, 0.0))
        id_hi, id_lo, _ = split3(jnp.where(mine[t : t + 1], local[t : t + 1], 0.0))
        extra = jnp.where(row == 0, t + 1.0, jnp.where(row == 1, id_hi, jnp.where(row == 2, id_lo, 0.0)))
        columns.append(jnp.concatenate([*split3(far_tiles[t]), extra], axis=0))
    picked = lax.dot_general(
        jnp.concatenate(columns, axis=1).astype(jnp.bfloat16),
        jnp.concatenate(chosen, axis=1).astype(jnp.bfloat16),
        (((1,), (1,)), ((), ())),
        preferred_element_type=jnp.float32,
    )
    label = picked[3 * ROWS : 3 * ROWS + 1]
    far_id = picked[3 * ROWS + 1 : 3 * ROWS + 2] + picked[3 * ROWS + 2 : 3 * ROWS + 3]
    info = jnp.concatenate([v[7:8] for v in far_tiles], axis=0)
    info = jnp.concatenate([info, jnp.zeros((TILE - tiles, TILE), jnp.float32)], axis=0).T
    of_tile = lax.broadcasted_iota(jnp.int32, (2 * SUB, TILE), 0).astype(jnp.float32) + 1.0
    lists = jnp.dot(
        info[: 2 * SUB, : 2 * SUB].astype(jnp.bfloat16),
        jnp.where(of_tile == label, 1.0, 0.0).astype(jnp.bfloat16),
        preferred_element_type=jnp.float32,
    )
    unused = jnp.logical_and(row == 2, label == 0.0)
    parts = [jnp.where(unused, 1.0, picked[:ROWS]), picked[ROWS : 2 * ROWS], picked[2 * ROWS : 3 * ROWS]]
    x3 = (parts[0] + parts[1] + parts[2])[2:3]

    far_vel = jnp.concatenate(gathered_pairs(table, count, lists, parts, x3, pairs) + [zeros], axis=0)

    place = lax.broadcasted_iota(jnp.int32, (hot.shape[1], TILE), 0).astype(jnp.float32)

    def seats(at):
        return jnp.where(place == at, 1.0, 0.0).astype(jnp.bfloat16)

    for j, e in enumerate([m] + peers):
        for t in range(tiles):
            hot[j, :, t * TILE : (t + 1) * TILE] = seats(ext[(half + e) * tiles + t][6:7] - first_id)

    slots = [m] + peers
    row = lax.broadcasted_iota(jnp.int32, (ROWS, TILE), 0)
    slot_lane = lax.broadcasted_iota(jnp.int32, (ROWS, TILE), 1).astype(jnp.float32)
    source = jnp.zeros((ROWS, hot.shape[1]), jnp.float32)
    for j in range(len(slots)):
        names = [jnp.where(row == 0, slot_lane, j * tiles + t + 1.0) for t in range(tiles)]
        source = source + lax.dot_general(
            jnp.concatenate(names, axis=1).astype(jnp.bfloat16),
            hot[j],
            (((1,), (1,)), ((), ())),
            preferred_element_type=jnp.float32,
        )
    body_all = lax.dot_general(
        jnp.where(label == 0.0, 0.0, far_vel).astype(jnp.bfloat16),
        seats(jnp.where(label == 0.0, -1.0, far_id)),
        (((1,), (1,)), ((), ())),
        preferred_element_type=jnp.float32,
    )
    spans = [slice(k, k + TILE) for k in range(0, hot.shape[1], TILE)]
    from_lane = [jnp.broadcast_to(source[:1, span].astype(jnp.int32), (ROWS, TILE)) for span in spans]
    from_name = [jnp.broadcast_to(source[1:2, span], (ROWS, TILE)) for span in spans]
    body_all = jnp.concatenate([body_all, jnp.zeros((ROWS - VROWS, hot.shape[1]), jnp.float32)], axis=0)
    seated = [body_all[:, span] for span in spans]

    def seat(j, seated):
        values = vel[slots[j]]
        values = jnp.concatenate([values, jnp.zeros((ROWS - VROWS, blobs), jnp.float32)], axis=0)
        for t in range(tiles):
            tile = values[:, t * TILE : (t + 1) * TILE]
            seated = [
                jnp.where(name == j * tiles + t + 1.0, jnp.take_along_axis(tile, at, axis=1), old)
                for name, at, old in zip(from_name, from_lane, seated)
            ]
        return seated

    seated = seat(0, seated)

    for e in peers:
        sized(vel.at[e], local_sem.at[3], vel_sem.at[e]).wait_recv()

    for j in range(1, len(slots)):
        seated = seat(j, seated)
    body_all = jnp.concatenate(seated, axis=1)[:VROWS]
    order = 3 * pb
    total = -(-order // TILE) * TILE
    body_all = jnp.concatenate([body_all, jnp.zeros((VROWS, total - hot.shape[1]), jnp.float32)], axis=1)
    lane = lax.broadcasted_iota(jnp.int32, (VROWS, total), 1)
    parts = [
        jnp.where(jnp.logical_and(lane >= k * pb, lane < (k + 1) * pb), body_all, 0.0) for k in range(own_plates)
    ]
    bodies = []
    for k in range(own_plates):
        body = jnp.zeros((1, total), jnp.float32)
        for c in range(3):
            shift = (c - k) * pb % total
            body = body + (pltpu.roll(parts[k], shift, 1) if shift else parts[k])[c : c + 1]
        bodies.append(body[:, :order])
    body_out[...] = jnp.concatenate(bodies, axis=0).astype(jnp.bfloat16)

    sized(block(0, n_member - 1), local_sem.at[0], data_sem.at[0]).wait_send()
    sized(vel.at[pl.ds(0, n_member - 2)], local_sem.at[3], vel_sem.at[0]).wait_send()

    @pl.when(jnp.logical_or(to_high, to_low))
    def _():
        sized(block(0, n_member), local_sem.at[1], data_sem.at[1]).wait_send()


def finish(vel_ref, body_ref, vel_out, body_out):
    vel_out[...] = vel_ref[...]
    body_out[...] = body_ref[...]


def on_device(n_region, n_member, positions, forces, blob_platelet, blob_rank, owner, pair_list, pair_count, pre):
    blobs = positions.shape[1]
    tiles = blobs // TILE
    own_plates, order, _ = pre.shape
    pb = order // 3
    seats = -(-own_plates * pb // TILE) * TILE
    depth = -(-3 * (2 * n_member * tiles + ROWS) // TILE) * TILE
    far = pl.BlockSpec(memory_space=pltpu.HBM)
    vector = pl.BlockSpec(memory_space=pltpu.VMEM)
    velocity, body_in = pl.pallas_call(
        functools.partial(kernel, n_region, n_member, pb, own_plates),
        out_shape=(
            pltpu.VMEM((3, blobs), jnp.float32),
            pltpu.VMEM((own_plates, order), jnp.bfloat16),
        ),
        in_specs=[far] * 7,
        out_specs=(vector, vector),
        scratch_shapes=[
            pltpu.VMEM((3, blobs), jnp.float32),
            pltpu.VMEM((3, blobs), jnp.float32),
            pltpu.VMEM((1, blobs), jnp.int32),
            pltpu.VMEM((1, blobs), jnp.int32),
            pltpu.SMEM(owner.shape, jnp.int32),
            pltpu.SMEM(pair_list.shape, jnp.int32),
            pltpu.SMEM(pair_count.shape, jnp.int32),
            pltpu.VMEM((2 * n_member * tiles + 1, ROWS, TILE), jnp.float32),
            pltpu.VMEM((2 * n_member * tiles + 1, DEPTH, TILE), jnp.bfloat16),
            pltpu.VMEM((tiles, PLANES * TILE, DEPTH), jnp.bfloat16),
            pltpu.VMEM((3 * tiles, TILE, TILE), jnp.float32),
            pltpu.VMEM((3 * tiles, TILE, TILE), jnp.float32),
            pltpu.VMEM((GATHER * TILE, depth), jnp.bfloat16),
            pltpu.VMEM((n_member, VROWS, blobs), jnp.float32),
            pltpu.VMEM((n_member - 1, seats, blobs), jnp.bfloat16),
            pltpu.SemaphoreType.DMA((7,)),
            pltpu.SemaphoreType.DMA((3,)),
            pltpu.SemaphoreType.DMA((n_member,)),
        ],
        compiler_params=pltpu.CompilerParams(collective_id=0, has_side_effects=True),
    )(
        positions,
        forces,
        blob_platelet,
        blob_rank,
        owner,
        pair_list,
        pair_count,
    )
    body_velocity = jnp.einsum("pab,pb->pa", pre, body_in, preferred_element_type=jnp.float32)
    return pl.pallas_call(
        finish,
        out_shape=(
            jax.ShapeDtypeStruct(velocity.shape, jnp.float32),
            jax.ShapeDtypeStruct(body_velocity.shape, jnp.float32),
        ),
        in_specs=[vector, vector],
        out_specs=(vector, vector),
        compiler_params=pltpu.CompilerParams(vmem_limit_bytes=1024 * 1024),
    )(velocity, body_velocity)


def solution(mesh):
    placed = (
        P(None, ("region", "member")),
        P(None, ("region", "member")),
        P(("region", "member")),
        P(("region", "member")),
        P("region"),
        P(("region", "member"), None),
        P(("region", "member")),
        P(("region", "member"), None, None),
    )
    return jax.shard_map(
        functools.partial(on_device, mesh.shape["region"], mesh.shape["member"]),
        mesh=mesh,
        in_specs=placed,
        out_specs=(P(None, ("region", "member")), P(("region", "member"), None)),
        check_vma=False,
    )
```

```python
import functools
import math

import jax
import jax.numpy as jnp
from jax import lax
from jax.experimental import pallas as pl
from jax.experimental.pallas import tpu as pltpu
from jax.sharding import PartitionSpec as P

TILE = 128
SUB = 8
VROWS = 4
ROWS = 8
PLANES = 4
DEPTH = 64
GATHER = 7
SCALE = 1.0 / (8.0 * math.pi)
MESH = pl.DeviceIdType.MESH


def split3(v):
    hi = v.astype(jnp.bfloat16).astype(jnp.float32)
    rest = v - hi
    mid = rest.astype(jnp.bfloat16).astype(jnp.float32)
    return hi, mid, rest - mid


def target_table(x):
    zero = jnp.zeros((1, TILE), jnp.float32)
    one = jnp.ones((1, TILE), jnp.float32)
    squares = jnp.sum(x * x, axis=0, keepdims=True)

    def plane(rows, tail=(), fixed=None):
        parts = list(zip(*[split3(v) for v in rows]))
        fixed = (zero, zero) if fixed is None else fixed
        blocks = []
        for k, part in enumerate((0, 0, 0, 1, 1, 2)):
            blocks += list(parts[part]) + (list(fixed) if k < 3 else [zero, zero])
        tail = list(split3(tail)) if len(tail) else [zero] * 3
        blocks += tail + [zero] * (DEPTH - len(blocks) - 3)
        blocks += [zero] * (TILE - DEPTH)
        return jnp.concatenate(blocks, axis=0).T[:, :DEPTH]

    x1, x2, x3 = x[0:1], x[1:2], x[2:3]
    none = [zero] * 3
    planes = [
        plane([-2.0 * x1, -2.0 * x2, -2.0 * x3] + none, squares + 1.0, (one, zero)),
        plane([-2.0 * x1, -2.0 * x2, 2.0 * x3] + none, squares, (one, zero)),
        plane(none + [x1, x2, x3], (), (zero, -one)),
        plane(none + [3.0 * x1, 3.0 * x2, -3.0 * x3], (), (zero, -3.0 * one)),
    ]
    rows = [p[b : b + SUB] for b in range(0, TILE, SUB) for p in planes]
    return jnp.concatenate(rows, axis=0).astype(jnp.bfloat16)


def source_table(rows, middle):
    row = lax.broadcasted_iota(jnp.int32, (SUB, TILE), 0)
    near = rows - middle
    squares = near * near
    products = near * pltpu.roll(near, SUB - 3, 0)

    def summed(v, at):
        v = v + pltpu.roll(v, SUB - 1, 0) + pltpu.roll(v, SUB - 2, 0)
        return pltpu.roll(v, at, 0)

    near = jnp.where(row == 6, summed(squares, 6), jnp.where(row == 7, summed(products, 7), near))
    hi, mid, lo = split3(near)
    ones = jnp.where(row < 3, 1.0, 0.0)
    spare = jnp.zeros((DEPTH - 7 * SUB, TILE), jnp.float32)
    return jnp.concatenate([hi, mid, lo, hi, mid, hi, ones, spare], axis=0).astype(jnp.bfloat16)


def gather_table(ext, count, table):
    section = lax.broadcasted_iota(jnp.int32, (3 * ROWS, TILE), 0) % ROWS
    spare = jnp.zeros((table.shape[1] - 3 * count - 3 * ROWS, TILE), jnp.float32)
    none = jnp.zeros((3 * ROWS, TILE), jnp.float32)
    turned = []
    for p, (c, factor) in enumerate(((0, -1.0), (1, -1.0), (2, -1.0), (2, 2.0), (3, 1.0), (4, 1.0), (5, 1.0))):
        parts = split3(ext[pl.ds(0, count), c, :] * factor)
        ones = jnp.where(section == p, 1.0, 0.0) if p < 3 else none
        turned.append(jnp.concatenate([*parts, ones, spare], axis=0).T)
    rows = [v[b : b + SUB] for b in range(0, TILE, SUB) for v in turned]
    table[...] = jnp.concatenate(rows, axis=0).astype(jnp.bfloat16)


def gathered_pairs(table, count, lists, parts, x3, pairs):
    x3 = jnp.broadcast_to(x3, (SUB, TILE))
    x3d = x3 + x3
    total = [jnp.zeros((SUB, TILE), jnp.float32)] * 3
    tile = lax.broadcasted_iota(jnp.int32, (count, TILE), 0).astype(jnp.float32)
    spare = jnp.zeros((table.shape[1] - 3 * count - 3 * ROWS, TILE), jnp.float32)
    for first in range(0, pairs, 2):
        columns = []
        for s in range(first, first + 2):
            chosen = jnp.where(lists[pairs : pairs + 1] > s, lists[s : s + 1], -1.0)
            hot = jnp.where(tile == chosen, 1.0, 0.0)
            columns.append(jnp.concatenate([hot, hot, hot, *parts, spare], axis=0))
        columns = jnp.concatenate(columns, axis=1).astype(jnp.bfloat16)
        planes = jnp.dot(table[...], columns, preferred_element_type=jnp.float32)
        for side in range(2):
            for b in range(TILE // SUB):
                d1, d2, d3, h2, f1, f2, f3 = [
                    planes[(b * GATHER + p) * SUB :][:SUB, side * TILE : (side + 1) * TILE] for p in range(GATHER)
                ]
                dd = d1 * d1 + d2 * d2 + d3 * d3
                c = h2 * x3
                w = lax.rsqrt(dd + 1.0)
                p = lax.rsqrt(dd + (c + c))
                w3 = w * w * w
                p2 = p * p
                p3 = p2 * p
                full = d1 * f1 + d2 * f2 + d3 * f3
                mirror = full - x3d * f3
                cp3 = c * p3
                alpha = (w + w3) - (p + cp3)
                gamma = 3.0 * (cp3 * p2) * mirror
                both = full * (w3 - p3) + gamma
                total[0] = total[0] + (f1 * alpha + d1 * both)
                total[1] = total[1] + (f2 * alpha + d2 * both)
                total[2] = total[2] + (f3 * alpha + d3 * both + h2 * gamma)
    return [jnp.sum(v, axis=0, keepdims=True) for v in total]


def kernel(
    n_region,
    n_member,
    pb,
    own_plates,
    pos_hbm,
    force_hbm,
    plate_hbm,
    rank_hbm,
    owner_hbm,
    list_hbm,
    count_hbm,
    vel_out,
    body_out,
    pos,
    force,
    plate,
    rank,
    owner_ref,
    list_ref,
    count_ref,
    ext,
    sources,
    targets,
    tgt,
    acc,
    table,
    vel,
    hot,
    found,
    local_sem,
    data_sem,
):
    r = lax.axis_index("region")
    m = lax.axis_index("member")
    half = n_member // 2
    tiles = pos.shape[1] // TILE
    blobs = pos.shape[1]
    plates = owner_ref.shape[0]
    pairs = list_ref.shape[1]
    has_low = r > 0
    has_high = r < n_region - 1
    to_high = jnp.logical_and(m >= half, has_high)
    to_low = jnp.logical_and(m < half, has_low)
    base = (half + m) * tiles

    far = n_member - 1 - m
    lower = jnp.where(m < half, m, far)

    def peer(j):
        mate = lax.rem(lower + 1 + j // 2, half)
        return jnp.where(j % 2 == 0, mate, n_member - 1 - mate)

    peers = [peer(j) for j in range(n_member - 2)]
    others = [far] + peers

    barrier = pltpu.get_barrier_semaphore()
    for e in others:
        pl.semaphore_signal(barrier, inc=1, device_id=(r, e), device_id_type=MESH)

    loads = [
        pltpu.make_async_copy(a, b, local_sem.at[i])
        for i, (a, b) in enumerate(
            ((pos_hbm, pos), (force_hbm, force), (plate_hbm, plate.at[0]), (rank_hbm, rank.at[0]),
             (owner_hbm, owner_ref), (list_hbm, list_ref), (count_hbm, count_ref))
        )
    ]
    for load in loads[:3]:
        load.start()

    @pl.when(has_low)
    def _():
        for k in range(half):
            pl.semaphore_signal(barrier, inc=1, device_id=(r - 1, half + k), device_id_type=MESH)

    @pl.when(has_high)
    def _():
        for k in range(half):
            pl.semaphore_signal(barrier, inc=1, device_id=(r + 1, k), device_id_type=MESH)

    for load in loads[3:]:
        load.start()

    for load in loads:
        load.wait()

    live = plate[...] < plates
    place_row = pos[...]
    push_row = force[...] * jnp.where(live, SCALE, 0.0)
    plate_row = plate[...]
    slot_of = jnp.zeros_like(plate_row)
    for k in range(plates):
        slot_of = jnp.where(plate_row == k, owner_ref[k], slot_of)
    body_at = jnp.where(live, slot_of * pb + rank[...], plates * pb).astype(jnp.float32)
    lane = lax.broadcasted_iota(jnp.int32, (1, TILE), 1)
    for t in range(tiles):
        span = slice(t * TILE, (t + 1) * TILE)
        info = jnp.where(lane == pairs, count_ref[t], 0)
        for s in range(pairs):
            info = jnp.where(lane == s, list_ref[t, s], info)
        ext[base + t] = jnp.concatenate(
            [place_row[:, span], push_row[:, span], body_at[:, span], info.astype(jnp.float32)], axis=0
        )

    def block(e, count=1):
        return ext.at[pl.ds(e * tiles, count * tiles)]

    def move(src, dst, send, recv, to):
        return pltpu.make_async_remote_copy(
            src_ref=src, dst_ref=dst, send_sem=send, recv_sem=recv, device_id=to, device_id_type=MESH
        )

    def near_copy(e):
        here = block(half + m)
        return move(here, here, local_sem.at[0], data_sem.at[0], (r, e))

    def rim_copy(k, shift, e, sem):
        return move(block(half + m), block(e), local_sem.at[1], data_sem.at[sem], (r + shift, lax.rem(m + k, n_member)))

    def sized(ref, send, recv):
        return move(ref, ref, send, recv, (r, far))

    rim_sends = jnp.where(jnp.logical_or(to_high, to_low), n_member, 0)
    pl.semaphore_wait(barrier, n_member - 1 + rim_sends)

    for late, early in zip(peers + [far], [far] + peers):
        near_copy(jnp.where(lower == 0, late, early)).start()

    @pl.when(to_high)
    def _():
        for k in range(n_member):
            rim_copy(k, 1, m - half, 1).start()

    @pl.when(to_low)
    def _():
        for k in range(n_member):
            rim_copy(k, -1, half + n_member + m, 2).start()

    @pl.when(jnp.logical_not(has_low))
    def _():
        ext[pl.ds(0, half * tiles)] = jnp.zeros((half * tiles, ROWS, TILE), jnp.float32)

    @pl.when(jnp.logical_not(has_high))
    def _():
        ext[pl.ds((half + n_member) * tiles, half * tiles)] = jnp.zeros(
            (half * tiles, ROWS, TILE), jnp.float32
        )

    across = lax.broadcasted_iota(jnp.int32, (ROWS, TILE), 0) < 2
    middle = jnp.where(across, jnp.broadcast_to(ext[base][:, :1], (ROWS, TILE)), 0.0)
    last = ext.shape[0] - 1
    ext[last] = jnp.zeros((ROWS, TILE), jnp.float32)
    sources[last] = source_table(jnp.zeros((ROWS, TILE), jnp.float32), middle)

    def tabulate(first, count):
        @pl.loop(0, count)
        def _(i):
            for t in range(tiles):
                at = first + i * tiles + t
                sources[at] = source_table(ext[at], middle)

    tabulate(base, 1)
    for t in range(tiles):
        own = place_row[:, t * TILE : (t + 1) * TILE]
        for c in range(3):
            tgt[t * 3 + c] = jnp.broadcast_to(own[c : c + 1], (TILE, TILE)).T
        targets[t] = target_table(own - middle[:3])

    def some_pairs(t, tile_ids, first):
        columns = jnp.concatenate([sources[e] for e in tile_ids], axis=1)
        planes = jnp.dot(targets[t], columns, preferred_element_type=jnp.float32)
        for side, e in enumerate(tile_ids):
            rows = ext[e]
            y1, y2, h, f1, f2, f3 = [jnp.broadcast_to(rows[c : c + 1], (SUB, TILE)) for c in range(6)]
            h2 = h + h
            for b in range(TILE // SUB):
                at = pl.ds(b * SUB, SUB)
                near, image, full, mirror = [
                    planes[(b * PLANES + p) * SUB :][:SUB, side * TILE : (side + 1) * TILE]
                    for p in range(PLANES)
                ]
                d1 = tgt[t * 3, at] - y1
                d2 = tgt[t * 3 + 1, at] - y2
                x3 = tgt[t * 3 + 2, at]
                d3 = x3 - h
                w = lax.rsqrt(near)
                p = lax.rsqrt(image)
                w3 = w * w * w
                p2 = p * p
                p3 = p2 * p
                cp3 = (h2 * x3) * p3
                alpha = (w + w3) - (p + cp3)
                gamma = cp3 * p2 * mirror
                both = full * (w3 - p3) + gamma
                terms = (f1 * alpha + d1 * both, f2 * alpha + d2 * both, f3 * alpha + d3 * both + h2 * gamma)
                for k in range(3):
                    if first:
                        acc[t * 3 + k, at] = terms[k]
                    else:
                        acc[t * 3 + k, at] = acc[t * 3 + k, at] + terms[k]

    @pl.loop(0, tiles)
    def _(t):
        some_pairs(t, [base + t], True)

    first_id = (m * (own_plates * pb)).astype(jnp.float32)
    place = lax.broadcasted_iota(jnp.int32, (hot.shape[1], TILE), 0).astype(jnp.float32)
    slots = [m] + peers
    name_row = lax.broadcasted_iota(jnp.int32, (ROWS, TILE), 0)
    slot_lane = lax.broadcasted_iota(jnp.int32, (ROWS, TILE), 1).astype(jnp.float32)

    def seats(at):
        return jnp.where(place == at, 1.0, 0.0).astype(jnp.bfloat16)

    def find(j):
        for t in range(tiles):
            hot[j, :, t * TILE : (t + 1) * TILE] = seats(ext[(half + slots[j]) * tiles + t][6:7] - first_id)
        names = [jnp.where(name_row == 0, slot_lane, j * tiles + t + 1.0) for t in range(tiles)]
        return lax.dot_general(
            jnp.concatenate(names, axis=1).astype(jnp.bfloat16),
            hot[j],
            (((1,), (1,)), ((), ())),
            preferred_element_type=jnp.float32,
        )

    found[...] = find(0)

    @pl.when(has_low)
    def _():
        sized(block(0, half), local_sem.at[0], data_sem.at[1]).wait_recv()

    @pl.when(has_high)
    def _():
        sized(block(0, half), local_sem.at[0], data_sem.at[2]).wait_recv()

    tabulate(0, half)
    tabulate((half + n_member) * tiles, half)
    sized(block(0, n_member - 1), local_sem.at[0], data_sem.at[0]).wait_recv()

    for e in others:
        tabulate((half + e) * tiles, 1)

    zeros = jnp.zeros((VROWS - 3, TILE), jnp.float32)

    def vel_copy(e):
        return move(vel.at[m], vel.at[m], local_sem.at[3], data_sem.at[3], (r, e))

    blocks = []
    for t in range(tiles):
        for s in range(1, pairs, 2):
            chosen = [jnp.where(k < count_ref[t], list_ref[t, k], last) for k in range(s, min(s + 2, pairs))]
            some_pairs(t, chosen, False)
        blocks.append([jnp.sum(acc[t * 3 + c].T, axis=0, keepdims=True) for c in range(3)] + [zeros])
    rows = jnp.concatenate([jnp.concatenate(block, axis=0) for block in blocks], axis=1)
    vel[m] = rows
    for e in peers:
        vel_copy(e).start()
    vel_out[...] = rows[:3]

    count = 2 * n_member * tiles
    gather_table(ext, count, table)

    room = own_plates * pb
    far_tiles = [ext[(half + far) * tiles + t] for t in range(tiles)]
    local = jnp.concatenate([v[6:7] for v in far_tiles], axis=0) - first_id
    mine = jnp.logical_and(local >= 0.0, local < float(room))
    counted = jnp.concatenate(
        [mine.astype(jnp.float32), jnp.zeros((2 * SUB - tiles, TILE), jnp.float32)], axis=0
    ).astype(jnp.bfloat16)
    up_to = lax.broadcasted_iota(jnp.int32, (TILE, TILE), 0) <= lax.broadcasted_iota(jnp.int32, (TILE, TILE), 1)
    order_in = jnp.dot(
        counted, jnp.where(up_to, 1.0, 0.0).astype(jnp.bfloat16), preferred_element_type=jnp.float32
    )
    seat = lax.broadcasted_iota(jnp.int32, (TILE, TILE), 0).astype(jnp.float32)
    row = lax.broadcasted_iota(jnp.int32, (ROWS, TILE), 0)
    before = jnp.full((1, 1), -1.0, jnp.float32)
    chosen, columns = [], []
    for t in range(tiles):
        at = jnp.where(mine[t : t + 1], order_in[t : t + 1] + before, -1.0)
        before = before + order_in[t : t + 1, TILE - 1 :]
        chosen.append(jnp.where(seat == at, 1.0, 0.0))
        id_hi, id_lo, _ = split3(jnp.where(mine[t : t + 1], local[t : t + 1], 0.0))
        extra = jnp.where(row == 0, t + 1.0, jnp.where(row == 1, id_hi, jnp.where(row == 2, id_lo, 0.0)))
        columns.append(jnp.concatenate([*split3(far_tiles[t]), extra], axis=0))
    picked = lax.dot_general(
        jnp.concatenate(columns, axis=1).astype(jnp.bfloat16),
        jnp.concatenate(chosen, axis=1).astype(jnp.bfloat16),
        (((1,), (1,)), ((), ())),
        preferred_element_type=jnp.float32,
    )
    label = picked[3 * ROWS : 3 * ROWS + 1]
    far_id = picked[3 * ROWS + 1 : 3 * ROWS + 2] + picked[3 * ROWS + 2 : 3 * ROWS + 3]
    info = jnp.concatenate([v[7:8] for v in far_tiles], axis=0)
    info = jnp.concatenate([info, jnp.zeros((TILE - tiles, TILE), jnp.float32)], axis=0).T
    of_tile = lax.broadcasted_iota(jnp.int32, (2 * SUB, TILE), 0).astype(jnp.float32) + 1.0
    lists = jnp.dot(
        info[: 2 * SUB, : 2 * SUB].astype(jnp.bfloat16),
        jnp.where(of_tile == label, 1.0, 0.0).astype(jnp.bfloat16),
        preferred_element_type=jnp.float32,
    )
    unused = jnp.logical_and(row == 2, label == 0.0)
    parts = [jnp.where(unused, 1.0, picked[:ROWS]), picked[ROWS : 2 * ROWS], picked[2 * ROWS : 3 * ROWS]]
    x3 = (parts[0] + parts[1] + parts[2])[2:3]

    far_vel = jnp.concatenate(gathered_pairs(table, count, lists, parts, x3, pairs) + [zeros], axis=0)

    order = 3 * pb
    total = -(-order // TILE) * TILE
    source = found[...]
    for j in range(1, len(slots)):
        source = source + find(j)

    def spread(v, k, fill):
        v = jnp.concatenate([v, jnp.zeros((v.shape[0], total - v.shape[1]), jnp.float32)], axis=1)
        lane = lax.broadcasted_iota(jnp.int32, v.shape, 1)
        v = jnp.where(jnp.logical_and(lane >= k * pb, lane < (k + 1) * pb), v, fill)
        shifts = [(c - k) * pb % total for c in range(3)]
        return [pltpu.roll(v, shift, 1) if shift else v for shift in shifts]

    body_all = lax.dot_general(
        jnp.where(label == 0.0, 0.0, far_vel).astype(jnp.bfloat16),
        seats(jnp.where(label == 0.0, -1.0, far_id)),
        (((1,), (1,)), ((), ())),
        preferred_element_type=jnp.float32,
    )
    part_of = lax.broadcasted_iota(jnp.int32, (1, total), 1)
    part_of = [part_of < (c + 1) * pb for c in range(3)]
    spans = [slice(k, k + TILE) for k in range(0, total, TILE)]
    from_lane, from_name, body = [], [], []
    for k in range(own_plates):
        table_k = spread(source, k, 0.0)
        table_k = table_k[0] + table_k[1] + table_k[2]
        from_lane += [jnp.broadcast_to(table_k[:1, v].astype(jnp.int32), (ROWS, TILE)) for v in spans]
        from_name += [jnp.broadcast_to(table_k[1:2, v], (ROWS, TILE)) for v in spans]
        fixed = spread(body_all, k, 0.0)
        fixed = fixed[0][0:1] + fixed[1][1:2] + fixed[2][2:3]
        body += [jnp.broadcast_to(fixed[:, v], (ROWS, TILE)) for v in spans]

    def seat(j, body):
        values = jnp.concatenate([vel[slots[j]], jnp.zeros((ROWS - VROWS, blobs), jnp.float32)], axis=0)
        for t in range(tiles):
            tile = values[:, t * TILE : (t + 1) * TILE]
            body = [
                jnp.where(name == j * tiles + t + 1.0, jnp.take_along_axis(tile, at, axis=1), old)
                for name, at, old in zip(from_name, from_lane, body)
            ]
        return body

    body = seat(0, body)

    sized(vel.at[pl.ds(0, n_member - 2)], local_sem.at[3], data_sem.at[3]).wait_recv()

    for j in range(1, len(slots)):
        body = seat(j, body)
    bodies = []
    for k in range(own_plates):
        rows = jnp.concatenate(body[k * len(spans) : (k + 1) * len(spans)], axis=1)
        row = jnp.where(part_of[0], rows[0:1], jnp.where(part_of[1], rows[1:2], rows[2:3]))
        bodies.append(row[:, :order])
    body_out[...] = jnp.concatenate(bodies, axis=0).astype(jnp.bfloat16)

    sized(block(0, n_member - 1), local_sem.at[0], data_sem.at[0]).wait_send()
    sized(vel.at[pl.ds(0, n_member - 2)], local_sem.at[3], data_sem.at[3]).wait_send()

    @pl.when(jnp.logical_or(to_high, to_low))
    def _():
        sized(block(0, n_member), local_sem.at[1], data_sem.at[1]).wait_send()


def finish(vel_ref, body_ref, vel_out, body_out):
    vel_out[...] = vel_ref[...]
    body_out[...] = body_ref[...]


def on_device(n_region, n_member, positions, forces, blob_platelet, blob_rank, owner, pair_list, pair_count, pre):
    blobs = positions.shape[1]
    tiles = blobs // TILE
    own_plates, order, _ = pre.shape
    pb = order // 3
    seats = -(-own_plates * pb // TILE) * TILE
    depth = -(-3 * (2 * n_member * tiles + ROWS) // TILE) * TILE
    far = pl.BlockSpec(memory_space=pltpu.HBM)
    vector = pl.BlockSpec(memory_space=pltpu.VMEM)
    velocity, body_in = pl.pallas_call(
        functools.partial(kernel, n_region, n_member, pb, own_plates),
        out_shape=(
            pltpu.VMEM((3, blobs), jnp.float32),
            pltpu.VMEM((own_plates, order), jnp.bfloat16),
        ),
        in_specs=[far] * 7,
        out_specs=(vector, vector),
        scratch_shapes=[
            pltpu.VMEM((3, blobs), jnp.float32),
            pltpu.VMEM((3, blobs), jnp.float32),
            pltpu.VMEM((1, blobs), jnp.int32),
            pltpu.VMEM((1, blobs), jnp.int32),
            pltpu.SMEM(owner.shape, jnp.int32),
            pltpu.SMEM(pair_list.shape, jnp.int32),
            pltpu.SMEM(pair_count.shape, jnp.int32),
            pltpu.VMEM((2 * n_member * tiles + 1, ROWS, TILE), jnp.float32),
            pltpu.VMEM((2 * n_member * tiles + 1, DEPTH, TILE), jnp.bfloat16),
            pltpu.VMEM((tiles, PLANES * TILE, DEPTH), jnp.bfloat16),
            pltpu.VMEM((3 * tiles, TILE, TILE), jnp.float32),
            pltpu.VMEM((3 * tiles, TILE, TILE), jnp.float32),
            pltpu.VMEM((GATHER * TILE, depth), jnp.bfloat16),
            pltpu.VMEM((n_member, VROWS, blobs), jnp.float32),
            pltpu.VMEM((n_member - 1, seats, blobs), jnp.bfloat16),
            pltpu.VMEM((ROWS, seats), jnp.float32),
            pltpu.SemaphoreType.DMA((7,)),
            pltpu.SemaphoreType.DMA((4,)),
        ],
        compiler_params=pltpu.CompilerParams(collective_id=0, has_side_effects=True),
    )(
        positions,
        forces,
        blob_platelet,
        blob_rank,
        owner,
        pair_list,
        pair_count,
    )
    body_velocity = jnp.einsum("pab,pb->pa", pre, body_in, preferred_element_type=jnp.float32)
    return pl.pallas_call(
        finish,
        out_shape=(
            jax.ShapeDtypeStruct(velocity.shape, jnp.float32),
            jax.ShapeDtypeStruct(body_velocity.shape, jnp.float32),
        ),
        in_specs=[vector, vector],
        out_specs=(vector, vector),
        compiler_params=pltpu.CompilerParams(vmem_limit_bytes=1024 * 1024),
    )(velocity, body_velocity)


def solution(mesh):
    placed = (
        P(None, ("region", "member")),
        P(None, ("region", "member")),
        P(("region", "member")),
        P(("region", "member")),
        P("region"),
        P(("region", "member"), None),
        P(("region", "member")),
        P(("region", "member"), None, None),
    )
    return jax.shard_map(
        functools.partial(on_device, mesh.shape["region"], mesh.shape["member"]),
        mesh=mesh,
        in_specs=placed,
        out_specs=(P(None, ("region", "member")), P(("region", "member"), None)),
        check_vma=False,
    )
```

```python
import functools
import math

import jax
import jax.numpy as jnp
from jax import lax
from jax.experimental import pallas as pl
from jax.experimental.pallas import tpu as pltpu
from jax.sharding import PartitionSpec as P

TILE = 128
SUB = 8
VROWS = 4
ROWS = 8
PLANES = 5
DEPTH = 64
GATHER = 7
SCALE = 1.0 / (8.0 * math.pi)
MESH = pl.DeviceIdType.MESH


def split3(v):
    hi = v.astype(jnp.bfloat16).astype(jnp.float32)
    rest = v - hi
    mid = rest.astype(jnp.bfloat16).astype(jnp.float32)
    return hi, mid, rest - mid


def target_table(x):
    zero = jnp.zeros((1, TILE), jnp.float32)
    one = jnp.ones((1, TILE), jnp.float32)
    squares = jnp.sum(x * x, axis=0, keepdims=True)

    def plane(rows, tail=(), fixed=None):
        parts = list(zip(*[split3(v) for v in rows]))
        fixed = (zero, zero) if fixed is None else fixed
        blocks = []
        for k, part in enumerate((0, 0, 0, 1, 1, 2)):
            blocks += list(parts[part]) + (list(fixed) if k < 3 else [zero, zero])
        tail = list(split3(tail)) if len(tail) else [zero] * 3
        blocks += tail + [zero] * (DEPTH - len(blocks) - 3)
        blocks += [zero] * (TILE - DEPTH)
        return jnp.concatenate(blocks, axis=0).T[:, :DEPTH]

    x1, x2, x3 = x[0:1], x[1:2], x[2:3]
    none = [zero] * 3
    planes = [
        plane([-2.0 * x1, -2.0 * x2, -2.0 * x3] + none, squares + 1.0, (one, zero)),
        plane([-2.0 * x1, -2.0 * x2, 2.0 * x3] + none, squares, (one, zero)),
        plane([zero, zero, 2.0 * x3] + none),
        plane(none + [x1, x2, x3], (), (zero, -one)),
        plane(none + [3.0 * x1, 3.0 * x2, -3.0 * x3], (), (zero, -3.0 * one)),
    ]
    rows = [p[b : b + SUB] for b in range(0, TILE, SUB) for p in planes]
    return jnp.concatenate(rows, axis=0).astype(jnp.bfloat16)


def source_table(rows, middle):
    row = lax.broadcasted_iota(jnp.int32, (SUB, TILE), 0)
    near = rows - middle
    squares = near * near
    products = near * pltpu.roll(near, SUB - 3, 0)

    def summed(v, at):
        v = v + pltpu.roll(v, SUB - 1, 0) + pltpu.roll(v, SUB - 2, 0)
        return pltpu.roll(v, at, 0)

    near = jnp.where(row == 6, summed(squares, 6), jnp.where(row == 7, summed(products, 7), near))
    hi, mid, lo = split3(near)
    ones = jnp.where(row < 3, 1.0, 0.0)
    spare = jnp.zeros((DEPTH - 7 * SUB, TILE), jnp.float32)
    return jnp.concatenate([hi, mid, lo, hi, mid, hi, ones, spare], axis=0).astype(jnp.bfloat16)


def gather_table(ext, count, table):
    section = lax.broadcasted_iota(jnp.int32, (3 * ROWS, TILE), 0) % ROWS
    spare = jnp.zeros((table.shape[1] - 3 * count - 3 * ROWS, TILE), jnp.float32)
    none = jnp.zeros((3 * ROWS, TILE), jnp.float32)
    turned = []
    for p, (c, factor) in enumerate(((0, -1.0), (1, -1.0), (2, -1.0), (2, 2.0), (3, 1.0), (4, 1.0), (5, 1.0))):
        parts = split3(ext[pl.ds(0, count), c, :] * factor)
        ones = jnp.where(section == p, 1.0, 0.0) if p < 3 else none
        turned.append(jnp.concatenate([*parts, ones, spare], axis=0).T)
    rows = [v[b : b + SUB] for b in range(0, TILE, SUB) for v in turned]
    table[...] = jnp.concatenate(rows, axis=0).astype(jnp.bfloat16)


def gathered_pairs(table, count, lists, parts, x3, pairs):
    x3 = jnp.broadcast_to(x3, (SUB, TILE))
    x3d = x3 + x3
    total = [jnp.zeros((SUB, TILE), jnp.float32)] * 3
    tile = lax.broadcasted_iota(jnp.int32, (count, TILE), 0).astype(jnp.float32)
    spare = jnp.zeros((table.shape[1] - 3 * count - 3 * ROWS, TILE), jnp.float32)
    for first in range(0, pairs, 2):
        columns = []
        for s in range(first, first + 2):
            chosen = jnp.where(lists[pairs : pairs + 1] > s, lists[s : s + 1], -1.0)
            hot = jnp.where(tile == chosen, 1.0, 0.0)
            columns.append(jnp.concatenate([hot, hot, hot, *parts, spare], axis=0))
        columns = jnp.concatenate(columns, axis=1).astype(jnp.bfloat16)
        planes = jnp.dot(table[...], columns, preferred_element_type=jnp.float32)
        for side in range(2):
            for b in range(TILE // SUB):
                d1, d2, d3, h2, f1, f2, f3 = [
                    planes[(b * GATHER + p) * SUB :][:SUB, side * TILE : (side + 1) * TILE] for p in range(GATHER)
                ]
                dd = d1 * d1 + d2 * d2 + d3 * d3
                c = h2 * x3
                w = lax.rsqrt(dd + 1.0)
                p = lax.rsqrt(dd + (c + c))
                w3 = w * w * w
                p2 = p * p
                p3 = p2 * p
                full = d1 * f1 + d2 * f2 + d3 * f3
                mirror = full - x3d * f3
                cp3 = c * p3
                alpha = (w + w3) - (p + cp3)
                gamma = 3.0 * (cp3 * p2) * mirror
                both = full * (w3 - p3) + gamma
                total[0] = total[0] + (f1 * alpha + d1 * both)
                total[1] = total[1] + (f2 * alpha + d2 * both)
                total[2] = total[2] + (f3 * alpha + d3 * both + h2 * gamma)
    return [jnp.sum(v, axis=0, keepdims=True) for v in total]


def kernel(
    n_region,
    n_member,
    pb,
    own_plates,
    pos_hbm,
    force_hbm,
    plate_hbm,
    rank_hbm,
    owner_hbm,
    list_hbm,
    count_hbm,
    vel_out,
    body_out,
    pos,
    force,
    plate,
    rank,
    owner_ref,
    list_ref,
    count_ref,
    ext,
    sources,
    targets,
    tgt,
    acc,
    table,
    vel,
    hot,
    found,
    local_sem,
    data_sem,
    far_ready,
):
    r = lax.axis_index("region")
    m = lax.axis_index("member")
    half = n_member // 2
    tiles = pos.shape[1] // TILE
    blobs = pos.shape[1]
    plates = owner_ref.shape[0]
    pairs = list_ref.shape[1]
    has_low = r > 0
    has_high = r < n_region - 1
    to_high = jnp.logical_and(m >= half, has_high)
    to_low = jnp.logical_and(m < half, has_low)
    base = (half + m) * tiles

    far = n_member - 1 - m
    lower = jnp.where(m < half, m, far)

    def peer(j):
        mate = lax.rem(lower + 1 + j // 2, half)
        return jnp.where(j % 2 == 0, mate, n_member - 1 - mate)

    peers = [peer(j) for j in range(n_member - 2)]
    others = [far] + peers

    barrier = pltpu.get_barrier_semaphore()
    first_end, last_end = m == 0, m == n_member - 1

    @pl.when(jnp.logical_not(last_end))
    def _():
        pl.semaphore_signal(barrier, inc=1, device_id=(r, far), device_id_type=MESH)

    for e in peers:
        pl.semaphore_signal(barrier, inc=1, device_id=(r, e), device_id_type=MESH)

    loads = [
        pltpu.make_async_copy(a, b, local_sem.at[i])
        for i, (a, b) in enumerate(
            ((pos_hbm, pos), (force_hbm, force), (plate_hbm, plate.at[0]), (rank_hbm, rank.at[0]),
             (owner_hbm, owner_ref), (list_hbm, list_ref), (count_hbm, count_ref))
        )
    ]
    for load in loads[:3]:
        load.start()

    @pl.when(has_low)
    def _():
        for k in range(half):
            pl.semaphore_signal(barrier, inc=1, device_id=(r - 1, half + k), device_id_type=MESH)

    @pl.when(has_high)
    def _():
        for k in range(half):
            pl.semaphore_signal(barrier, inc=1, device_id=(r + 1, k), device_id_type=MESH)

    for load in loads[3:]:
        load.start()

    for load in loads:
        load.wait()

    live = plate[...] < plates
    place_row = pos[...]
    push_row = force[...] * jnp.where(live, SCALE, 0.0)
    plate_row = plate[...]
    slot_of = jnp.zeros_like(plate_row)
    for k in range(plates):
        slot_of = jnp.where(plate_row == k, owner_ref[k], slot_of)
    body_at = jnp.where(live, slot_of * pb + rank[...], plates * pb).astype(jnp.float32)
    lane = lax.broadcasted_iota(jnp.int32, (1, TILE), 1)
    for t in range(tiles):
        span = slice(t * TILE, (t + 1) * TILE)
        info = jnp.where(lane == pairs, count_ref[t], 0)
        for s in range(pairs):
            info = jnp.where(lane == s, list_ref[t, s], info)
        ext[base + t] = jnp.concatenate(
            [place_row[:, span], push_row[:, span], body_at[:, span], info.astype(jnp.float32)], axis=0
        )

    def block(e, count=1):
        return ext.at[pl.ds(e * tiles, count * tiles)]

    def move(src, dst, send, recv, to):
        return pltpu.make_async_remote_copy(
            src_ref=src, dst_ref=dst, send_sem=send, recv_sem=recv, device_id=to, device_id_type=MESH
        )

    def near_copy(e):
        here = block(half + m)
        return move(here, here, local_sem.at[0], data_sem.at[0], (r, e))

    def rim_copy(k, shift, e, sem):
        return move(block(half + m), block(e), local_sem.at[1], data_sem.at[sem], (r + shift, lax.rem(m + k, n_member)))

    def sized(ref, send, recv):
        return move(ref, ref, send, recv, (r, far))

    rim_sends = jnp.where(jnp.logical_or(to_high, to_low), n_member, 0)
    pl.semaphore_wait(barrier, n_member - 1 + rim_sends - jnp.where(first_end, 1, 0))

    @pl.when(last_end)
    def _():
        pl.semaphore_signal(far_ready, inc=1, device_id=(r, far), device_id_type=MESH)

    turns = [jnp.where(lower == 0, late, early) for late, early in zip(peers + [far], [far] + peers)]
    for e in turns[:-1]:
        near_copy(e).start()

    @pl.when(jnp.logical_not(first_end))
    def _():
        near_copy(turns[-1]).start()

    @pl.when(to_high)
    def _():
        for k in range(n_member):
            rim_copy(k, 1, m - half, 1).start()

    @pl.when(to_low)
    def _():
        for k in range(n_member):
            rim_copy(k, -1, half + n_member + m, 2).start()

    @pl.when(jnp.logical_not(has_low))
    def _():
        ext[pl.ds(0, half * tiles)] = jnp.zeros((half * tiles, ROWS, TILE), jnp.float32)

    @pl.when(jnp.logical_not(has_high))
    def _():
        ext[pl.ds((half + n_member) * tiles, half * tiles)] = jnp.zeros(
            (half * tiles, ROWS, TILE), jnp.float32
        )

    across = lax.broadcasted_iota(jnp.int32, (ROWS, TILE), 0) < 2
    middle = jnp.where(across, jnp.broadcast_to(ext[base][:, :1], (ROWS, TILE)), 0.0)
    last = ext.shape[0] - 1
    ext[last] = jnp.zeros((ROWS, TILE), jnp.float32)
    sources[last] = source_table(jnp.zeros((ROWS, TILE), jnp.float32), middle)

    def tabulate(first, count):
        @pl.loop(0, count)
        def _(i):
            for t in range(tiles):
                at = first + i * tiles + t
                sources[at] = source_table(ext[at], middle)

    tabulate(base, 1)
    for t in range(tiles):
        own = place_row[:, t * TILE : (t + 1) * TILE]
        for c in range(3):
            tgt[t * 3 + c] = jnp.broadcast_to(own[c : c + 1], (TILE, TILE)).T
        targets[t] = target_table(own - middle[:3])

    def some_pairs(t, tile_ids, first):
        columns = jnp.concatenate([sources[e] for e in tile_ids], axis=1)
        planes = jnp.dot(targets[t], columns, preferred_element_type=jnp.float32)
        for side, e in enumerate(tile_ids):
            rows = ext[e]
            y1, y2, h, f1, f2, f3 = [jnp.broadcast_to(rows[c : c + 1], (SUB, TILE)) for c in range(6)]
            h2 = h + h
            for b in range(TILE // SUB):
                at = pl.ds(b * SUB, SUB)
                near, image, c, full, mirror = [
                    planes[(b * PLANES + p) * SUB :][:SUB, side * TILE : (side + 1) * TILE]
                    for p in range(PLANES)
                ]
                d1 = tgt[t * 3, at] - y1
                d2 = tgt[t * 3 + 1, at] - y2
                x3 = tgt[t * 3 + 2, at]
                d3 = x3 - h
                w = lax.rsqrt(near)
                p = lax.rsqrt(image)
                w3 = w * w * w
                p2 = p * p
                p3 = p2 * p
                cp3 = c * p3
                alpha = (w + w3) - (p + cp3)
                gamma = cp3 * p2 * mirror
                both = full * (w3 - p3) + gamma
                terms = (f1 * alpha + d1 * both, f2 * alpha + d2 * both, f3 * alpha + d3 * both + h2 * gamma)
                for k in range(3):
                    if first:
                        acc[t * 3 + k, at] = terms[k]
                    else:
                        acc[t * 3 + k, at] = acc[t * 3 + k, at] + terms[k]

    @pl.loop(0, tiles)
    def _(t):
        some_pairs(t, [base + t], True)

    first_id = (m * (own_plates * pb)).astype(jnp.float32)
    place = lax.broadcasted_iota(jnp.int32, (hot.shape[1], TILE), 0).astype(jnp.float32)
    slots = [m] + peers
    name_row = lax.broadcasted_iota(jnp.int32, (ROWS, TILE), 0)
    slot_lane = lax.broadcasted_iota(jnp.int32, (ROWS, TILE), 1).astype(jnp.float32)

    def seats(at):
        return jnp.where(place == at, 1.0, 0.0).astype(jnp.bfloat16)

    def find(j):
        for t in range(tiles):
            hot[j, :, t * TILE : (t + 1) * TILE] = seats(ext[(half + slots[j]) * tiles + t][6:7] - first_id)
        names = [jnp.where(name_row == 0, slot_lane, j * tiles + t + 1.0) for t in range(tiles)]
        return lax.dot_general(
            jnp.concatenate(names, axis=1).astype(jnp.bfloat16),
            hot[j],
            (((1,), (1,)), ((), ())),
            preferred_element_type=jnp.float32,
        )

    found[...] = find(0)

    @pl.when(first_end)
    def _():
        pl.semaphore_wait(far_ready, 1)
        near_copy(far).start()

    @pl.when(has_low)
    def _():
        sized(block(0, half), local_sem.at[0], data_sem.at[1]).wait_recv()

    @pl.when(has_high)
    def _():
        sized(block(0, half), local_sem.at[0], data_sem.at[2]).wait_recv()

    tabulate(0, half)
    tabulate((half + n_member) * tiles, half)
    sized(block(0, n_member - 1), local_sem.at[0], data_sem.at[0]).wait_recv()

    for e in others:
        for t in range(tiles):
            at = (half + e) * tiles + t
            sources[at] = source_table(ext[at], middle)

    zeros = jnp.zeros((VROWS - 3, TILE), jnp.float32)

    def vel_copy(e):
        return move(vel.at[m], vel.at[m], local_sem.at[3], data_sem.at[3], (r, e))

    blocks = []
    for t in range(tiles):
        for s in range(1, pairs, 2):
            chosen = [jnp.where(k < count_ref[t], list_ref[t, k], last) for k in range(s, min(s + 2, pairs))]
            some_pairs(t, chosen, False)
        blocks.append([jnp.sum(acc[t * 3 + c].T, axis=0, keepdims=True) for c in range(3)] + [zeros])
    rows = jnp.concatenate([jnp.concatenate(block, axis=0) for block in blocks], axis=1)
    vel[m] = rows
    for e in peers:
        vel_copy(e).start()
    vel_out[...] = rows[:3]

    count = 2 * n_member * tiles
    gather_table(ext, count, table)

    room = own_plates * pb
    far_tiles = [ext[(half + far) * tiles + t] for t in range(tiles)]
    local = jnp.concatenate([v[6:7] for v in far_tiles], axis=0) - first_id
    mine = jnp.logical_and(local >= 0.0, local < float(room))
    counted = jnp.concatenate(
        [mine.astype(jnp.float32), jnp.zeros((2 * SUB - tiles, TILE), jnp.float32)], axis=0
    ).astype(jnp.bfloat16)
    up_to = lax.broadcasted_iota(jnp.int32, (TILE, TILE), 0) <= lax.broadcasted_iota(jnp.int32, (TILE, TILE), 1)
    order_in = jnp.dot(
        counted, jnp.where(up_to, 1.0, 0.0).astype(jnp.bfloat16), preferred_element_type=jnp.float32
    )
    seat = lax.broadcasted_iota(jnp.int32, (TILE, TILE), 0).astype(jnp.float32)
    row = lax.broadcasted_iota(jnp.int32, (ROWS, TILE), 0)
    before = jnp.full((1, 1), -1.0, jnp.float32)
    chosen, columns = [], []
    for t in range(tiles):
        at = jnp.where(mine[t : t + 1], order_in[t : t + 1] + before, -1.0)
        before = before + order_in[t : t + 1, TILE - 1 :]
        chosen.append(jnp.where(seat == at, 1.0, 0.0))
        id_hi, id_lo, _ = split3(jnp.where(mine[t : t + 1], local[t : t + 1], 0.0))
        extra = jnp.where(row == 0, t + 1.0, jnp.where(row == 1, id_hi, jnp.where(row == 2, id_lo, 0.0)))
        columns.append(jnp.concatenate([*split3(far_tiles[t]), extra], axis=0))
    picked = lax.dot_general(
        jnp.concatenate(columns, axis=1).astype(jnp.bfloat16),
        jnp.concatenate(chosen, axis=1).astype(jnp.bfloat16),
        (((1,), (1,)), ((), ())),
        preferred_element_type=jnp.float32,
    )
    label = picked[3 * ROWS : 3 * ROWS + 1]
    far_id = picked[3 * ROWS + 1 : 3 * ROWS + 2] + picked[3 * ROWS + 2 : 3 * ROWS + 3]
    info = jnp.concatenate([v[7:8] for v in far_tiles], axis=0)
    info = jnp.concatenate([info, jnp.zeros((TILE - tiles, TILE), jnp.float32)], axis=0).T
    of_tile = lax.broadcasted_iota(jnp.int32, (2 * SUB, TILE), 0).astype(jnp.float32) + 1.0
    lists = jnp.dot(
        info[: 2 * SUB, : 2 * SUB].astype(jnp.bfloat16),
        jnp.where(of_tile == label, 1.0, 0.0).astype(jnp.bfloat16),
        preferred_element_type=jnp.float32,
    )
    unused = jnp.logical_and(row == 2, label == 0.0)
    parts = [jnp.where(unused, 1.0, picked[:ROWS]), picked[ROWS : 2 * ROWS], picked[2 * ROWS : 3 * ROWS]]
    x3 = (parts[0] + parts[1] + parts[2])[2:3]

    far_vel = jnp.concatenate(gathered_pairs(table, count, lists, parts, x3, pairs) + [zeros], axis=0)

    order = 3 * pb
    total = -(-order // TILE) * TILE
    source = found[...]
    for j in range(1, len(slots)):
        source = source + find(j)

    def spread(v, k, fill):
        v = jnp.concatenate([v, jnp.zeros((v.shape[0], total - v.shape[1]), jnp.float32)], axis=1)
        lane = lax.broadcasted_iota(jnp.int32, v.shape, 1)
        v = jnp.where(jnp.logical_and(lane >= k * pb, lane < (k + 1) * pb), v, fill)
        shifts = [(c - k) * pb % total for c in range(3)]
        return [pltpu.roll(v, shift, 1) if shift else v for shift in shifts]

    body_all = lax.dot_general(
        jnp.where(label == 0.0, 0.0, far_vel).astype(jnp.bfloat16),
        seats(jnp.where(label == 0.0, -1.0, far_id)),
        (((1,), (1,)), ((), ())),
        preferred_element_type=jnp.float32,
    )
    part_of = lax.broadcasted_iota(jnp.int32, (1, total), 1)
    part_of = [part_of < (c + 1) * pb for c in range(3)]
    spans = [slice(k, k + TILE) for k in range(0, total, TILE)]
    from_lane, from_name, body = [], [], []
    for k in range(own_plates):
        table_k = spread(source, k, 0.0)
        table_k = table_k[0] + table_k[1] + table_k[2]
        from_lane += [jnp.broadcast_to(table_k[:1, v].astype(jnp.int32), (ROWS, TILE)) for v in spans]
        from_name += [jnp.broadcast_to(table_k[1:2, v], (ROWS, TILE)) for v in spans]
        fixed = spread(body_all, k, 0.0)
        fixed = fixed[0][0:1] + fixed[1][1:2] + fixed[2][2:3]
        body += [jnp.broadcast_to(fixed[:, v], (ROWS, TILE)) for v in spans]

    def seat(j, body):
        values = jnp.concatenate([vel[slots[j]], jnp.zeros((ROWS - VROWS, blobs), jnp.float32)], axis=0)
        for t in range(tiles):
            tile = values[:, t * TILE : (t + 1) * TILE]
            body = [
                jnp.where(name == j * tiles + t + 1.0, jnp.take_along_axis(tile, at, axis=1), old)
                for name, at, old in zip(from_name, from_lane, body)
            ]
        return body

    body = seat(0, body)

    sized(vel.at[pl.ds(0, n_member - 2)], local_sem.at[3], data_sem.at[3]).wait_recv()

    for j in range(1, len(slots)):
        body = seat(j, body)
    bodies = []
    for k in range(own_plates):
        rows = jnp.concatenate(body[k * len(spans) : (k + 1) * len(spans)], axis=1)
        row = jnp.where(part_of[0], rows[0:1], jnp.where(part_of[1], rows[1:2], rows[2:3]))
        bodies.append(row[:, :order])
    body_out[...] = jnp.concatenate(bodies, axis=0).astype(jnp.bfloat16)

    sized(block(0, n_member - 1), local_sem.at[0], data_sem.at[0]).wait_send()
    sized(vel.at[pl.ds(0, n_member - 2)], local_sem.at[3], data_sem.at[3]).wait_send()

    @pl.when(jnp.logical_or(to_high, to_low))
    def _():
        sized(block(0, n_member), local_sem.at[1], data_sem.at[1]).wait_send()


def finish(vel_ref, body_ref, vel_out, body_out):
    vel_out[...] = vel_ref[...]
    body_out[...] = body_ref[...]


def on_device(n_region, n_member, positions, forces, blob_platelet, blob_rank, owner, pair_list, pair_count, pre):
    blobs = positions.shape[1]
    tiles = blobs // TILE
    own_plates, order, _ = pre.shape
    pb = order // 3
    seats = -(-own_plates * pb // TILE) * TILE
    depth = -(-3 * (2 * n_member * tiles + ROWS) // TILE) * TILE
    far = pl.BlockSpec(memory_space=pltpu.HBM)
    vector = pl.BlockSpec(memory_space=pltpu.VMEM)
    velocity, body_in = pl.pallas_call(
        functools.partial(kernel, n_region, n_member, pb, own_plates),
        out_shape=(
            pltpu.VMEM((3, blobs), jnp.float32),
            pltpu.VMEM((own_plates, order), jnp.bfloat16),
        ),
        in_specs=[far] * 7,
        out_specs=(vector, vector),
        scratch_shapes=[
            pltpu.VMEM((3, blobs), jnp.float32),
            pltpu.VMEM((3, blobs), jnp.float32),
            pltpu.VMEM((1, blobs), jnp.int32),
            pltpu.VMEM((1, blobs), jnp.int32),
            pltpu.SMEM(owner.shape, jnp.int32),
            pltpu.SMEM(pair_list.shape, jnp.int32),
            pltpu.SMEM(pair_count.shape, jnp.int32),
            pltpu.VMEM((2 * n_member * tiles + 1, ROWS, TILE), jnp.float32),
            pltpu.VMEM((2 * n_member * tiles + 1, DEPTH, TILE), jnp.bfloat16),
            pltpu.VMEM((tiles, PLANES * TILE, DEPTH), jnp.bfloat16),
            pltpu.VMEM((3 * tiles, TILE, TILE), jnp.float32),
            pltpu.VMEM((3 * tiles, TILE, TILE), jnp.float32),
            pltpu.VMEM((GATHER * TILE, depth), jnp.bfloat16),
            pltpu.VMEM((n_member, VROWS, blobs), jnp.float32),
            pltpu.VMEM((n_member - 1, seats, blobs), jnp.bfloat16),
            pltpu.VMEM((ROWS, seats), jnp.float32),
            pltpu.SemaphoreType.DMA((7,)),
            pltpu.SemaphoreType.DMA((4,)),
            pltpu.SemaphoreType.REGULAR,
        ],
        compiler_params=pltpu.CompilerParams(collective_id=0, has_side_effects=True),
    )(
        positions,
        forces,
        blob_platelet,
        blob_rank,
        owner,
        pair_list,
        pair_count,
    )
    body_velocity = jnp.einsum("pab,pb->pa", pre, body_in, preferred_element_type=jnp.float32)
    return pl.pallas_call(
        finish,
        out_shape=(
            jax.ShapeDtypeStruct(velocity.shape, jnp.float32),
            jax.ShapeDtypeStruct(body_velocity.shape, jnp.float32),
        ),
        in_specs=[vector, vector],
        out_specs=(vector, vector),
        compiler_params=pltpu.CompilerParams(vmem_limit_bytes=1024 * 1024),
    )(velocity, body_velocity)


def solution(mesh):
    placed = (
        P(None, ("region", "member")),
        P(None, ("region", "member")),
        P(("region", "member")),
        P(("region", "member")),
        P("region"),
        P(("region", "member"), None),
        P(("region", "member")),
        P(("region", "member"), None, None),
    )
    return jax.shard_map(
        functools.partial(on_device, mesh.shape["region"], mesh.shape["member"]),
        mesh=mesh,
        in_specs=placed,
        out_specs=(P(None, ("region", "member")), P(("region", "member"), None)),
        check_vma=False,
    )
```

```python
import functools
import math

import jax
import jax.numpy as jnp
from jax import lax
from jax.experimental import pallas as pl
from jax.experimental.pallas import tpu as pltpu
from jax.sharding import PartitionSpec as P

TILE = 128
SUB = 8
VROWS = 4
ROWS = 8
PLANES = 5
DEPTH = 64
GATHER = 7
SCALE = 1.0 / (8.0 * math.pi)
MESH = pl.DeviceIdType.MESH


def pair_terms(x1, x2, x3, src):
    y1, y2, h, f1, f2, f3, h2 = src
    d1 = x1 - y1
    d2 = x2 - y2
    d3 = x3 - h
    r3 = x3 + h
    s = d1 * d1 + d2 * d2
    w = lax.rsqrt(s + d3 * d3 + 1.0)
    p = lax.rsqrt(s + r3 * r3)
    w3 = w * w * w
    p2 = p * p
    p3 = p2 * p
    along = d1 * f1 + d2 * f2
    full = along + d3 * f3
    mirror = along - r3 * f3
    cp3 = (h2 * x3) * p3
    alpha = (w + w3) - (p + cp3)
    gamma = 3.0 * (cp3 * p2) * mirror
    both = full * (w3 - p3) + gamma
    return (
        f1 * alpha + d1 * both,
        f2 * alpha + d2 * both,
        f3 * alpha + d3 * both + h2 * gamma,
    )


def split3(v):
    hi = v.astype(jnp.bfloat16).astype(jnp.float32)
    rest = v - hi
    mid = rest.astype(jnp.bfloat16).astype(jnp.float32)
    return hi, mid, rest - mid


def target_table(x):
    zero = jnp.zeros((1, TILE), jnp.float32)
    one = jnp.ones((1, TILE), jnp.float32)
    squares = jnp.sum(x * x, axis=0, keepdims=True)

    def plane(rows, tail=(), fixed=None):
        parts = list(zip(*[split3(v) for v in rows]))
        fixed = (zero, zero) if fixed is None else fixed
        blocks = []
        for k, part in enumerate((0, 0, 0, 1, 1, 2)):
            blocks += list(parts[part]) + (list(fixed) if k < 3 else [zero, zero])
        tail = list(split3(tail)) if len(tail) else [zero] * 3
        blocks += tail + [zero] * (DEPTH - len(blocks) - 3)
        blocks += [zero] * (TILE - DEPTH)
        return jnp.concatenate(blocks, axis=0).T[:, :DEPTH]

    x1, x2, x3 = x[0:1], x[1:2], x[2:3]
    none = [zero] * 3
    planes = [
        plane([-2.0 * x1, -2.0 * x2, -2.0 * x3] + none, squares + 1.0, (one, zero)),
        plane([-2.0 * x1, -2.0 * x2, 2.0 * x3] + none, squares, (one, zero)),
        plane([zero, zero, 2.0 * x3] + none),
        plane(none + [x1, x2, x3], (), (zero, -one)),
        plane(none + [3.0 * x1, 3.0 * x2, -3.0 * x3], (), (zero, -3.0 * one)),
    ]
    rows = [p[b : b + SUB] for b in range(0, TILE, SUB) for p in planes]
    return jnp.concatenate(rows, axis=0).astype(jnp.bfloat16)


def source_table(rows, middle):
    row = lax.broadcasted_iota(jnp.int32, (SUB, TILE), 0)
    near = rows - middle
    squares = near * near
    products = near * pltpu.roll(near, SUB - 3, 0)

    def summed(v, at):
        v = v + pltpu.roll(v, SUB - 1, 0) + pltpu.roll(v, SUB - 2, 0)
        return pltpu.roll(v, at, 0)

    near = jnp.where(row == 6, summed(squares, 6), jnp.where(row == 7, summed(products, 7), near))
    hi, mid, lo = split3(near)
    ones = jnp.where(row < 3, 1.0, 0.0)
    spare = jnp.zeros((DEPTH - 7 * SUB, TILE), jnp.float32)
    return jnp.concatenate([hi, mid, lo, hi, mid, hi, ones, spare], axis=0).astype(jnp.bfloat16)


def gather_table(ext, count, table):
    section = lax.broadcasted_iota(jnp.int32, (3 * ROWS, TILE), 0) % ROWS
    spare = jnp.zeros((table.shape[1] - 3 * count - 3 * ROWS, TILE), jnp.float32)
    none = jnp.zeros((3 * ROWS, TILE), jnp.float32)
    turned = []
    for p, (c, factor) in enumerate(((0, -1.0), (1, -1.0), (2, -1.0), (2, 2.0), (3, 1.0), (4, 1.0), (5, 1.0))):
        parts = split3(ext[pl.ds(0, count), c, :] * factor)
        ones = jnp.where(section == p, 1.0, 0.0) if p < 3 else none
        turned.append(jnp.concatenate([*parts, ones, spare], axis=0).T)
    rows = [v[b : b + SUB] for b in range(0, TILE, SUB) for v in turned]
    table[...] = jnp.concatenate(rows, axis=0).astype(jnp.bfloat16)


def gathered_pairs(table, count, lists, parts, x3, pairs):
    x3 = jnp.broadcast_to(x3, (SUB, TILE))
    x3d = x3 + x3
    total = [jnp.zeros((SUB, TILE), jnp.float32)] * 3
    tile = lax.broadcasted_iota(jnp.int32, (count, TILE), 0).astype(jnp.float32)
    spare = jnp.zeros((table.shape[1] - 3 * count - 3 * ROWS, TILE), jnp.float32)
    for first in range(0, pairs, 2):
        columns = []
        for s in range(first, first + 2):
            chosen = jnp.where(lists[pairs : pairs + 1] > s, lists[s : s + 1], -1.0)
            hot = jnp.where(tile == chosen, 1.0, 0.0)
            columns.append(jnp.concatenate([hot, hot, hot, *parts, spare], axis=0))
        columns = jnp.concatenate(columns, axis=1).astype(jnp.bfloat16)
        planes = jnp.dot(table[...], columns, preferred_element_type=jnp.float32)
        for side in range(2):
            for b in range(TILE // SUB):
                d1, d2, d3, h2, f1, f2, f3 = [
                    planes[(b * GATHER + p) * SUB :][:SUB, side * TILE : (side + 1) * TILE] for p in range(GATHER)
                ]
                dd = d1 * d1 + d2 * d2 + d3 * d3
                c = h2 * x3
                w = lax.rsqrt(dd + 1.0)
                p = lax.rsqrt(dd + (c + c))
                w3 = w * w * w
                p2 = p * p
                p3 = p2 * p
                full = d1 * f1 + d2 * f2 + d3 * f3
                mirror = full - x3d * f3
                cp3 = c * p3
                alpha = (w + w3) - (p + cp3)
                gamma = 3.0 * (cp3 * p2) * mirror
                both = full * (w3 - p3) + gamma
                total[0] = total[0] + (f1 * alpha + d1 * both)
                total[1] = total[1] + (f2 * alpha + d2 * both)
                total[2] = total[2] + (f3 * alpha + d3 * both + h2 * gamma)
    return [jnp.sum(v, axis=0, keepdims=True) for v in total]


def kernel(
    n_region,
    n_member,
    pb,
    own_plates,
    pos_hbm,
    force_hbm,
    plate_hbm,
    rank_hbm,
    owner_hbm,
    list_hbm,
    count_hbm,
    vel_out,
    body_out,
    pos,
    force,
    plate,
    rank,
    owner_ref,
    list_ref,
    count_ref,
    ext,
    sources,
    targets,
    tgt,
    acc,
    table,
    vel,
    hot,
    found,
    local_sem,
    data_sem,
    far_ready,
):
    r = lax.axis_index("region")
    m = lax.axis_index("member")
    half = n_member // 2
    tiles = pos.shape[1] // TILE
    blobs = pos.shape[1]
    plates = owner_ref.shape[0]
    pairs = list_ref.shape[1]
    has_low = r > 0
    has_high = r < n_region - 1
    to_high = jnp.logical_and(m >= half, has_high)
    to_low = jnp.logical_and(m < half, has_low)
    base = (half + m) * tiles

    far = n_member - 1 - m
    lower = jnp.where(m < half, m, far)

    def peer(j):
        mate = lax.rem(lower + 1 + j // 2, half)
        return jnp.where(j % 2 == 0, mate, n_member - 1 - mate)

    peers = [peer(j) for j in range(n_member - 2)]
    others = [far] + peers

    barrier = pltpu.get_barrier_semaphore()
    first_end, last_end = m == 0, m == n_member - 1

    @pl.when(jnp.logical_not(last_end))
    def _():
        pl.semaphore_signal(barrier, inc=1, device_id=(r, far), device_id_type=MESH)

    for e in peers:
        pl.semaphore_signal(barrier, inc=1, device_id=(r, e), device_id_type=MESH)

    loads = [
        pltpu.make_async_copy(a, b, local_sem.at[i])
        for i, (a, b) in enumerate(
            ((pos_hbm, pos), (force_hbm, force), (plate_hbm, plate.at[0]), (rank_hbm, rank.at[0]),
             (owner_hbm, owner_ref), (list_hbm, list_ref), (count_hbm, count_ref))
        )
    ]
    for load in loads[:3]:
        load.start()

    @pl.when(has_low)
    def _():
        for k in range(half):
            pl.semaphore_signal(barrier, inc=1, device_id=(r - 1, half + k), device_id_type=MESH)

    @pl.when(has_high)
    def _():
        for k in range(half):
            pl.semaphore_signal(barrier, inc=1, device_id=(r + 1, k), device_id_type=MESH)

    for load in loads[3:]:
        load.start()

    for load in loads:
        load.wait()

    live = plate[...] < plates
    place_row = pos[...]
    push_row = force[...] * jnp.where(live, SCALE, 0.0)
    plate_row = plate[...]
    slot_of = jnp.zeros_like(plate_row)
    for k in range(plates):
        slot_of = jnp.where(plate_row == k, owner_ref[k], slot_of)
    body_at = jnp.where(live, slot_of * pb + rank[...], plates * pb).astype(jnp.float32)
    lane = lax.broadcasted_iota(jnp.int32, (1, TILE), 1)
    for t in range(tiles):
        span = slice(t * TILE, (t + 1) * TILE)
        info = jnp.where(lane == pairs, count_ref[t], 0)
        for s in range(pairs):
            info = jnp.where(lane == s, list_ref[t, s], info)
        ext[base + t] = jnp.concatenate(
            [place_row[:, span], push_row[:, span], body_at[:, span], info.astype(jnp.float32)], axis=0
        )

    def block(e, count=1):
        return ext.at[pl.ds(e * tiles, count * tiles)]

    def move(src, dst, send, recv, to):
        return pltpu.make_async_remote_copy(
            src_ref=src, dst_ref=dst, send_sem=send, recv_sem=recv, device_id=to, device_id_type=MESH
        )

    def near_copy(e):
        here = block(half + m)
        return move(here, here, local_sem.at[0], data_sem.at[0], (r, e))

    def rim_copy(k, shift, e, sem):
        return move(block(half + m), block(e), local_sem.at[1], data_sem.at[sem], (r + shift, lax.rem(m + k, n_member)))

    def sized(ref, send, recv):
        return move(ref, ref, send, recv, (r, far))

    rim_sends = jnp.where(jnp.logical_or(to_high, to_low), n_member, 0)
    pl.semaphore_wait(barrier, n_member - 1 + rim_sends - jnp.where(first_end, 1, 0))

    @pl.when(last_end)
    def _():
        pl.semaphore_signal(far_ready, inc=1, device_id=(r, far), device_id_type=MESH)

    turns = [jnp.where(lower == 0, late, early) for late, early in zip(peers + [far], [far] + peers)]
    for e in turns[:-1]:
        near_copy(e).start()

    @pl.when(jnp.logical_not(first_end))
    def _():
        near_copy(turns[-1]).start()

    @pl.when(to_high)
    def _():
        for k in range(n_member):
            rim_copy(k, 1, m - half, 1).start()

    @pl.when(to_low)
    def _():
        for k in range(n_member):
            rim_copy(k, -1, half + n_member + m, 2).start()

    @pl.when(jnp.logical_not(has_low))
    def _():
        ext[pl.ds(0, half * tiles)] = jnp.zeros((half * tiles, ROWS, TILE), jnp.float32)

    @pl.when(jnp.logical_not(has_high))
    def _():
        ext[pl.ds((half + n_member) * tiles, half * tiles)] = jnp.zeros(
            (half * tiles, ROWS, TILE), jnp.float32
        )

    across = lax.broadcasted_iota(jnp.int32, (ROWS, TILE), 0) < 2
    middle = jnp.where(across, jnp.broadcast_to(ext[base][:, :1], (ROWS, TILE)), 0.0)
    last = ext.shape[0] - 1
    ext[last] = jnp.zeros((ROWS, TILE), jnp.float32)
    sources[last] = source_table(jnp.zeros((ROWS, TILE), jnp.float32), middle)

    def tabulate(first, count):
        @pl.loop(0, count)
        def _(i):
            for t in range(tiles):
                at = first + i * tiles + t
                sources[at] = source_table(ext[at], middle)

    tabulate(base, 1)
    for t in range(tiles):
        own = place_row[:, t * TILE : (t + 1) * TILE]
        for c in range(3):
            tgt[t * 3 + c] = jnp.broadcast_to(own[c : c + 1], (TILE, TILE)).T
        targets[t] = target_table(own - middle[:3])

    def some_pairs(t, tile_ids):
        columns = jnp.concatenate([sources[e] for e in tile_ids], axis=1)
        planes = jnp.dot(targets[t], columns, preferred_element_type=jnp.float32)
        for side, e in enumerate(tile_ids):
            rows = ext[e]
            y1, y2, h, f1, f2, f3 = [jnp.broadcast_to(rows[c : c + 1], (SUB, TILE)) for c in range(6)]
            h2 = h + h
            for b in range(TILE // SUB):
                at = pl.ds(b * SUB, SUB)
                near, image, c, full, mirror = [
                    planes[(b * PLANES + p) * SUB :][:SUB, side * TILE : (side + 1) * TILE]
                    for p in range(PLANES)
                ]
                d1 = tgt[t * 3, at] - y1
                d2 = tgt[t * 3 + 1, at] - y2
                x3 = tgt[t * 3 + 2, at]
                d3 = x3 - h
                w = lax.rsqrt(near)
                p = lax.rsqrt(image)
                w3 = w * w * w
                p2 = p * p
                p3 = p2 * p
                cp3 = c * p3
                alpha = (w + w3) - (p + cp3)
                gamma = cp3 * p2 * mirror
                both = full * (w3 - p3) + gamma
                terms = (f1 * alpha + d1 * both, f2 * alpha + d2 * both, f3 * alpha + d3 * both + h2 * gamma)
                for k in range(3):
                    acc[t * 3 + k, at] = acc[t * 3 + k, at] + terms[k]

    @pl.loop(0, tiles)
    def _(t):
        rows = ext[base + t]
        y1, y2, h, f1, f2, f3 = [jnp.broadcast_to(rows[c : c + 1], (SUB, TILE)) for c in range(6)]
        source = (y1, y2, h, f1, f2, f3, h + h)
        for b in range(TILE // SUB):
            at = pl.ds(b * SUB, SUB)
            terms = pair_terms(tgt[t * 3, at], tgt[t * 3 + 1, at], tgt[t * 3 + 2, at], source)
            for k in range(3):
                acc[t * 3 + k, at] = terms[k]

    first_id = (m * (own_plates * pb)).astype(jnp.float32)
    place = lax.broadcasted_iota(jnp.int32, (hot.shape[1], TILE), 0).astype(jnp.float32)
    slots = [m] + peers
    name_row = lax.broadcasted_iota(jnp.int32, (ROWS, TILE), 0)
    slot_lane = lax.broadcasted_iota(jnp.int32, (ROWS, TILE), 1).astype(jnp.float32)

    def seats(at):
        return jnp.where(place == at, 1.0, 0.0).astype(jnp.bfloat16)

    def find(j):
        for t in range(tiles):
            hot[j, :, t * TILE : (t + 1) * TILE] = seats(ext[(half + slots[j]) * tiles + t][6:7] - first_id)
        names = [jnp.where(name_row == 0, slot_lane, j * tiles + t + 1.0) for t in range(tiles)]
        return lax.dot_general(
            jnp.concatenate(names, axis=1).astype(jnp.bfloat16),
            hot[j],
            (((1,), (1,)), ((), ())),
            preferred_element_type=jnp.float32,
        )

    found[...] = find(0)

    @pl.when(first_end)
    def _():
        pl.semaphore_wait(far_ready, 1)
        near_copy(far).start()

    @pl.when(has_low)
    def _():
        sized(block(0, half), local_sem.at[0], data_sem.at[1]).wait_recv()

    @pl.when(has_high)
    def _():
        sized(block(0, half), local_sem.at[0], data_sem.at[2]).wait_recv()

    tabulate(0, half)
    tabulate((half + n_member) * tiles, half)
    sized(block(0, n_member - 1), local_sem.at[0], data_sem.at[0]).wait_recv()

    for e in others:
        for t in range(tiles):
            at = (half + e) * tiles + t
            sources[at] = source_table(ext[at], middle)

    zeros = jnp.zeros((VROWS - 3, TILE), jnp.float32)

    def vel_copy(e):
        return move(vel.at[m], vel.at[m], local_sem.at[3], data_sem.at[3], (r, e))

    blocks = []
    for t in range(tiles):
        for s in range(1, pairs, 2):
            chosen = [jnp.where(k < count_ref[t], list_ref[t, k], last) for k in range(s, min(s + 2, pairs))]
            some_pairs(t, chosen)
        blocks.append([jnp.sum(acc[t * 3 + c].T, axis=0, keepdims=True) for c in range(3)] + [zeros])
    rows = jnp.concatenate([jnp.concatenate(block, axis=0) for block in blocks], axis=1)
    vel[m] = rows
    for e in peers:
        vel_copy(e).start()
    vel_out[...] = rows[:3]

    count = 2 * n_member * tiles
    gather_table(ext, count, table)

    room = own_plates * pb
    far_tiles = [ext[(half + far) * tiles + t] for t in range(tiles)]
    local = jnp.concatenate([v[6:7] for v in far_tiles], axis=0) - first_id
    mine = jnp.logical_and(local >= 0.0, local < float(room))
    counted = jnp.concatenate(
        [mine.astype(jnp.float32), jnp.zeros((2 * SUB - tiles, TILE), jnp.float32)], axis=0
    ).astype(jnp.bfloat16)
    up_to = lax.broadcasted_iota(jnp.int32, (TILE, TILE), 0) <= lax.broadcasted_iota(jnp.int32, (TILE, TILE), 1)
    order_in = jnp.dot(
        counted, jnp.where(up_to, 1.0, 0.0).astype(jnp.bfloat16), preferred_element_type=jnp.float32
    )
    seat = lax.broadcasted_iota(jnp.int32, (TILE, TILE), 0).astype(jnp.float32)
    row = lax.broadcasted_iota(jnp.int32, (ROWS, TILE), 0)
    before = jnp.full((1, 1), -1.0, jnp.float32)
    chosen, columns = [], []
    for t in range(tiles):
        at = jnp.where(mine[t : t + 1], order_in[t : t + 1] + before, -1.0)
        before = before + order_in[t : t + 1, TILE - 1 :]
        chosen.append(jnp.where(seat == at, 1.0, 0.0))
        id_hi, id_lo, _ = split3(jnp.where(mine[t : t + 1], local[t : t + 1], 0.0))
        extra = jnp.where(row == 0, t + 1.0, jnp.where(row == 1, id_hi, jnp.where(row == 2, id_lo, 0.0)))
        columns.append(jnp.concatenate([*split3(far_tiles[t]), extra], axis=0))
    picked = lax.dot_general(
        jnp.concatenate(columns, axis=1).astype(jnp.bfloat16),
        jnp.concatenate(chosen, axis=1).astype(jnp.bfloat16),
        (((1,), (1,)), ((), ())),
        preferred_element_type=jnp.float32,
    )
    label = picked[3 * ROWS : 3 * ROWS + 1]
    far_id = picked[3 * ROWS + 1 : 3 * ROWS + 2] + picked[3 * ROWS + 2 : 3 * ROWS + 3]
    info = jnp.concatenate([v[7:8] for v in far_tiles], axis=0)
    info = jnp.concatenate([info, jnp.zeros((TILE - tiles, TILE), jnp.float32)], axis=0).T
    of_tile = lax.broadcasted_iota(jnp.int32, (2 * SUB, TILE), 0).astype(jnp.float32) + 1.0
    lists = jnp.dot(
        info[: 2 * SUB, : 2 * SUB].astype(jnp.bfloat16),
        jnp.where(of_tile == label, 1.0, 0.0).astype(jnp.bfloat16),
        preferred_element_type=jnp.float32,
    )
    unused = jnp.logical_and(row == 2, label == 0.0)
    parts = [jnp.where(unused, 1.0, picked[:ROWS]), picked[ROWS : 2 * ROWS], picked[2 * ROWS : 3 * ROWS]]
    x3 = (parts[0] + parts[1] + parts[2])[2:3]

    far_vel = jnp.concatenate(gathered_pairs(table, count, lists, parts, x3, pairs) + [zeros], axis=0)

    order = 3 * pb
    total = -(-order // TILE) * TILE
    source = found[...]
    for j in range(1, len(slots)):
        source = source + find(j)

    def spread(v, k, fill):
        v = jnp.concatenate([v, jnp.zeros((v.shape[0], total - v.shape[1]), jnp.float32)], axis=1)
        lane = lax.broadcasted_iota(jnp.int32, v.shape, 1)
        v = jnp.where(jnp.logical_and(lane >= k * pb, lane < (k + 1) * pb), v, fill)
        shifts = [(c - k) * pb % total for c in range(3)]
        return [pltpu.roll(v, shift, 1) if shift else v for shift in shifts]

    body_all = lax.dot_general(
        jnp.where(label == 0.0, 0.0, far_vel).astype(jnp.bfloat16),
        seats(jnp.where(label == 0.0, -1.0, far_id)),
        (((1,), (1,)), ((), ())),
        preferred_element_type=jnp.float32,
    )
    part_of = lax.broadcasted_iota(jnp.int32, (1, total), 1)
    part_of = [part_of < (c + 1) * pb for c in range(3)]
    spans = [slice(k, k + TILE) for k in range(0, total, TILE)]
    from_lane, from_name, body = [], [], []
    for k in range(own_plates):
        table_k = spread(source, k, 0.0)
        table_k = table_k[0] + table_k[1] + table_k[2]
        from_lane += [jnp.broadcast_to(table_k[:1, v].astype(jnp.int32), (ROWS, TILE)) for v in spans]
        from_name += [jnp.broadcast_to(table_k[1:2, v], (ROWS, TILE)) for v in spans]
        fixed = spread(body_all, k, 0.0)
        fixed = fixed[0][0:1] + fixed[1][1:2] + fixed[2][2:3]
        body += [jnp.broadcast_to(fixed[:, v], (ROWS, TILE)) for v in spans]

    def seat(j, body):
        values = jnp.concatenate([vel[slots[j]], jnp.zeros((ROWS - VROWS, blobs), jnp.float32)], axis=0)
        for t in range(tiles):
            tile = values[:, t * TILE : (t + 1) * TILE]
            body = [
                jnp.where(name == j * tiles + t + 1.0, jnp.take_along_axis(tile, at, axis=1), old)
                for name, at, old in zip(from_name, from_lane, body)
            ]
        return body

    body = seat(0, body)

    sized(vel.at[pl.ds(0, n_member - 2)], local_sem.at[3], data_sem.at[3]).wait_recv()

    for j in range(1, len(slots)):
        body = seat(j, body)
    bodies = []
    for k in range(own_plates):
        rows = jnp.concatenate(body[k * len(spans) : (k + 1) * len(spans)], axis=1)
        row = jnp.where(part_of[0], rows[0:1], jnp.where(part_of[1], rows[1:2], rows[2:3]))
        bodies.append(row[:, :order])
    body_out[...] = jnp.concatenate(bodies, axis=0).astype(jnp.bfloat16)

    sized(block(0, n_member - 1), local_sem.at[0], data_sem.at[0]).wait_send()
    sized(vel.at[pl.ds(0, n_member - 2)], local_sem.at[3], data_sem.at[3]).wait_send()

    @pl.when(jnp.logical_or(to_high, to_low))
    def _():
        sized(block(0, n_member), local_sem.at[1], data_sem.at[1]).wait_send()


def finish(vel_ref, body_ref, vel_out, body_out):
    vel_out[...] = vel_ref[...]
    body_out[...] = body_ref[...]


def on_device(n_region, n_member, positions, forces, blob_platelet, blob_rank, owner, pair_list, pair_count, pre):
    blobs = positions.shape[1]
    tiles = blobs // TILE
    own_plates, order, _ = pre.shape
    pb = order // 3
    seats = -(-own_plates * pb // TILE) * TILE
    depth = -(-3 * (2 * n_member * tiles + ROWS) // TILE) * TILE
    far = pl.BlockSpec(memory_space=pltpu.HBM)
    vector = pl.BlockSpec(memory_space=pltpu.VMEM)
    velocity, body_in = pl.pallas_call(
        functools.partial(kernel, n_region, n_member, pb, own_plates),
        out_shape=(
            pltpu.VMEM((3, blobs), jnp.float32),
            pltpu.VMEM((own_plates, order), jnp.bfloat16),
        ),
        in_specs=[far] * 7,
        out_specs=(vector, vector),
        scratch_shapes=[
            pltpu.VMEM((3, blobs), jnp.float32),
            pltpu.VMEM((3, blobs), jnp.float32),
            pltpu.VMEM((1, blobs), jnp.int32),
            pltpu.VMEM((1, blobs), jnp.int32),
            pltpu.SMEM(owner.shape, jnp.int32),
            pltpu.SMEM(pair_list.shape, jnp.int32),
            pltpu.SMEM(pair_count.shape, jnp.int32),
            pltpu.VMEM((2 * n_member * tiles + 1, ROWS, TILE), jnp.float32),
            pltpu.VMEM((2 * n_member * tiles + 1, DEPTH, TILE), jnp.bfloat16),
            pltpu.VMEM((tiles, PLANES * TILE, DEPTH), jnp.bfloat16),
            pltpu.VMEM((3 * tiles, TILE, TILE), jnp.float32),
            pltpu.VMEM((3 * tiles, TILE, TILE), jnp.float32),
            pltpu.VMEM((GATHER * TILE, depth), jnp.bfloat16),
            pltpu.VMEM((n_member, VROWS, blobs), jnp.float32),
            pltpu.VMEM((n_member - 1, seats, blobs), jnp.bfloat16),
            pltpu.VMEM((ROWS, seats), jnp.float32),
            pltpu.SemaphoreType.DMA((7,)),
            pltpu.SemaphoreType.DMA((4,)),
            pltpu.SemaphoreType.REGULAR,
        ],
        compiler_params=pltpu.CompilerParams(collective_id=0, has_side_effects=True),
    )(
        positions,
        forces,
        blob_platelet,
        blob_rank,
        owner,
        pair_list,
        pair_count,
    )
    body_velocity = jnp.einsum("pab,pb->pa", pre, body_in, preferred_element_type=jnp.float32)
    return pl.pallas_call(
        finish,
        out_shape=(
            jax.ShapeDtypeStruct(velocity.shape, jnp.float32),
            jax.ShapeDtypeStruct(body_velocity.shape, jnp.float32),
        ),
        in_specs=[vector, vector],
        out_specs=(vector, vector),
        compiler_params=pltpu.CompilerParams(vmem_limit_bytes=1024 * 1024),
    )(velocity, body_velocity)


def solution(mesh):
    placed = (
        P(None, ("region", "member")),
        P(None, ("region", "member")),
        P(("region", "member")),
        P(("region", "member")),
        P("region"),
        P(("region", "member"), None),
        P(("region", "member")),
        P(("region", "member"), None, None),
    )
    return jax.shard_map(
        functools.partial(on_device, mesh.shape["region"], mesh.shape["member"]),
        mesh=mesh,
        in_specs=placed,
        out_specs=(P(None, ("region", "member")), P(("region", "member"), None)),
        check_vma=False,
    )
```

```python
import functools
import math

import jax
import jax.numpy as jnp
from jax import lax
from jax.experimental import pallas as pl
from jax.experimental.pallas import tpu as pltpu
from jax.sharding import PartitionSpec as P

TILE = 128
SUB = 8
VROWS = 4
ROWS = 8
PLANES = 5
DEPTH = 64
GATHER = 7
SCALE = 1.0 / (8.0 * math.pi)
MESH = pl.DeviceIdType.MESH


def pair_terms(x1, x2, x3, src):
    y1, y2, h, f1, f2, f3, h2 = src
    d1 = x1 - y1
    d2 = x2 - y2
    d3 = x3 - h
    r3 = x3 + h
    s = d1 * d1 + d2 * d2
    w = lax.rsqrt(s + d3 * d3 + 1.0)
    p = lax.rsqrt(s + r3 * r3)
    w3 = w * w * w
    p2 = p * p
    p3 = p2 * p
    along = d1 * f1 + d2 * f2
    full = along + d3 * f3
    mirror = along - r3 * f3
    cp3 = (h2 * x3) * p3
    alpha = (w + w3) - (p + cp3)
    gamma = 3.0 * (cp3 * p2) * mirror
    both = full * (w3 - p3) + gamma
    return (
        f1 * alpha + d1 * both,
        f2 * alpha + d2 * both,
        f3 * alpha + d3 * both + h2 * gamma,
    )


def split3(v):
    hi = v.astype(jnp.bfloat16).astype(jnp.float32)
    rest = v - hi
    mid = rest.astype(jnp.bfloat16).astype(jnp.float32)
    return hi, mid, rest - mid


def target_table(x):
    zero = jnp.zeros((1, TILE), jnp.float32)
    one = jnp.ones((1, TILE), jnp.float32)
    squares = jnp.sum(x * x, axis=0, keepdims=True)

    def plane(rows, tail=(), fixed=None):
        parts = list(zip(*[split3(v) for v in rows]))
        fixed = (zero, zero) if fixed is None else fixed
        blocks = []
        for k, part in enumerate((0, 0, 0, 1, 1, 2)):
            blocks += list(parts[part]) + (list(fixed) if k < 3 else [zero, zero])
        tail = list(split3(tail)) if len(tail) else [zero] * 3
        blocks += tail + [zero] * (DEPTH - len(blocks) - 3)
        blocks += [zero] * (TILE - DEPTH)
        return jnp.concatenate(blocks, axis=0).T[:, :DEPTH]

    x1, x2, x3 = x[0:1], x[1:2], x[2:3]
    none = [zero] * 3
    planes = [
        plane([-2.0 * x1, -2.0 * x2, -2.0 * x3] + none, squares + 1.0, (one, zero)),
        plane([-2.0 * x1, -2.0 * x2, 2.0 * x3] + none, squares, (one, zero)),
        plane([zero, zero, 2.0 * x3] + none),
        plane(none + [x1, x2, x3], (), (zero, -one)),
        plane(none + [3.0 * x1, 3.0 * x2, -3.0 * x3], (), (zero, -3.0 * one)),
    ]
    rows = [p[b : b + SUB] for b in range(0, TILE, SUB) for p in planes]
    return jnp.concatenate(rows, axis=0).astype(jnp.bfloat16)


def source_table(rows, middle):
    row = lax.broadcasted_iota(jnp.int32, (SUB, TILE), 0)
    near = rows - middle
    squares = near * near
    products = near * pltpu.roll(near, SUB - 3, 0)

    def summed(v, at):
        v = v + pltpu.roll(v, SUB - 1, 0) + pltpu.roll(v, SUB - 2, 0)
        return pltpu.roll(v, at, 0)

    near = jnp.where(row == 6, summed(squares, 6), jnp.where(row == 7, summed(products, 7), near))
    hi, mid, lo = split3(near)
    ones = jnp.where(row < 3, 1.0, 0.0)
    spare = jnp.zeros((DEPTH - 7 * SUB, TILE), jnp.float32)
    return jnp.concatenate([hi, mid, lo, hi, mid, hi, ones, spare], axis=0).astype(jnp.bfloat16)


def gather_table(ext, count, table):
    section = lax.broadcasted_iota(jnp.int32, (3 * ROWS, TILE), 0) % ROWS
    spare = jnp.zeros((table.shape[1] - 3 * count - 3 * ROWS, TILE), jnp.float32)
    none = jnp.zeros((3 * ROWS, TILE), jnp.float32)
    turned = []
    for p, (c, factor) in enumerate(((0, -1.0), (1, -1.0), (2, -1.0), (2, 2.0), (3, 1.0), (4, 1.0), (5, 1.0))):
        parts = split3(ext[pl.ds(0, count), c, :] * factor)
        ones = jnp.where(section == p, 1.0, 0.0) if p < 3 else none
        turned.append(jnp.concatenate([*parts, ones, spare], axis=0).T)
    rows = [v[b : b + SUB] for b in range(0, TILE, SUB) for v in turned]
    table[...] = jnp.concatenate(rows, axis=0).astype(jnp.bfloat16)


def gathered_pairs(table, count, lists, parts, x3, pairs):
    x3 = jnp.broadcast_to(x3, (SUB, TILE))
    x3d = x3 + x3
    total = [jnp.zeros((SUB, TILE), jnp.float32)] * 3
    tile = lax.broadcasted_iota(jnp.int32, (count, TILE), 0).astype(jnp.float32)
    spare = jnp.zeros((table.shape[1] - 3 * count - 3 * ROWS, TILE), jnp.float32)
    for first in range(0, pairs, 2):
        columns = []
        for s in range(first, first + 2):
            chosen = jnp.where(lists[pairs : pairs + 1] > s, lists[s : s + 1], -1.0)
            hot = jnp.where(tile == chosen, 1.0, 0.0)
            columns.append(jnp.concatenate([hot, hot, hot, *parts, spare], axis=0))
        columns = jnp.concatenate(columns, axis=1).astype(jnp.bfloat16)
        planes = jnp.dot(table[...], columns, preferred_element_type=jnp.float32)
        for side in range(2):
            for b in range(TILE // SUB):
                d1, d2, d3, h2, f1, f2, f3 = [
                    planes[(b * GATHER + p) * SUB :][:SUB, side * TILE : (side + 1) * TILE] for p in range(GATHER)
                ]
                dd = d1 * d1 + d2 * d2 + d3 * d3
                c = h2 * x3
                w = lax.rsqrt(dd + 1.0)
                p = lax.rsqrt(dd + (c + c))
                w3 = w * w * w
                p2 = p * p
                p3 = p2 * p
                full = d1 * f1 + d2 * f2 + d3 * f3
                mirror = full - x3d * f3
                cp3 = c * p3
                alpha = (w + w3) - (p + cp3)
                gamma = 3.0 * (cp3 * p2) * mirror
                both = full * (w3 - p3) + gamma
                total[0] = total[0] + (f1 * alpha + d1 * both)
                total[1] = total[1] + (f2 * alpha + d2 * both)
                total[2] = total[2] + (f3 * alpha + d3 * both + h2 * gamma)
    return [jnp.sum(v, axis=0, keepdims=True) for v in total]


def kernel(
    n_region,
    n_member,
    pb,
    own_plates,
    pos_hbm,
    force_hbm,
    plate_hbm,
    rank_hbm,
    owner_hbm,
    list_hbm,
    count_hbm,
    vel_out,
    body_out,
    pos,
    force,
    plate,
    rank,
    owner_ref,
    list_ref,
    count_ref,
    ext,
    sources,
    targets,
    tgt,
    acc,
    table,
    vel,
    hot,
    found,
    local_sem,
    data_sem,
    far_ready,
):
    r = lax.axis_index("region")
    m = lax.axis_index("member")
    half = n_member // 2
    tiles = pos.shape[1] // TILE
    blobs = pos.shape[1]
    plates = owner_ref.shape[0]
    pairs = list_ref.shape[1]
    has_low = r > 0
    has_high = r < n_region - 1
    to_high = jnp.logical_and(m >= half, has_high)
    to_low = jnp.logical_and(m < half, has_low)
    base = (half + m) * tiles

    far = n_member - 1 - m
    lower = jnp.where(m < half, m, far)

    def peer(j):
        mate = lax.rem(lower + 1 + j // 2, half)
        return jnp.where(j % 2 == 0, mate, n_member - 1 - mate)

    peers = [peer(j) for j in range(n_member - 2)]
    others = [far] + peers

    barrier = pltpu.get_barrier_semaphore()
    first_end, last_end = m == 0, m == n_member - 1

    @pl.when(jnp.logical_not(last_end))
    def _():
        pl.semaphore_signal(barrier, inc=1, device_id=(r, far), device_id_type=MESH)

    for e in peers:
        pl.semaphore_signal(barrier, inc=1, device_id=(r, e), device_id_type=MESH)

    loads = [
        pltpu.make_async_copy(a, b, local_sem.at[i])
        for i, (a, b) in enumerate(
            ((pos_hbm, pos), (force_hbm, force), (plate_hbm, plate.at[0]), (rank_hbm, rank.at[0]),
             (owner_hbm, owner_ref), (list_hbm, list_ref), (count_hbm, count_ref))
        )
    ]
    for load in loads[:3]:
        load.start()

    @pl.when(has_low)
    def _():
        for k in range(half):
            pl.semaphore_signal(barrier, inc=1, device_id=(r - 1, half + k), device_id_type=MESH)

    @pl.when(has_high)
    def _():
        for k in range(half):
            pl.semaphore_signal(barrier, inc=1, device_id=(r + 1, k), device_id_type=MESH)

    for load in loads[3:]:
        load.start()

    for load in loads:
        load.wait()

    live = plate[...] < plates
    place_row = pos[...]
    push_row = force[...] * jnp.where(live, SCALE, 0.0)
    plate_row = plate[...]
    slot_of = jnp.zeros_like(plate_row)
    for k in range(plates):
        slot_of = jnp.where(plate_row == k, owner_ref[k], slot_of)
    body_at = jnp.where(live, slot_of * pb + rank[...], plates * pb).astype(jnp.float32)
    lane = lax.broadcasted_iota(jnp.int32, (1, TILE), 1)
    for t in range(tiles):
        span = slice(t * TILE, (t + 1) * TILE)
        info = jnp.where(lane == pairs, count_ref[t], 0)
        for s in range(pairs):
            info = jnp.where(lane == s, list_ref[t, s], info)
        ext[base + t] = jnp.concatenate(
            [place_row[:, span], push_row[:, span], body_at[:, span], info.astype(jnp.float32)], axis=0
        )

    def block(e, count=1):
        return ext.at[pl.ds(e * tiles, count * tiles)]

    def move(src, dst, send, recv, to):
        return pltpu.make_async_remote_copy(
            src_ref=src, dst_ref=dst, send_sem=send, recv_sem=recv, device_id=to, device_id_type=MESH
        )

    def near_copy(e):
        here = block(half + m)
        return move(here, here, local_sem.at[0], data_sem.at[0], (r, e))

    def rim_copy(k, shift, e, sem):
        return move(block(half + m), block(e), local_sem.at[1], data_sem.at[sem], (r + shift, lax.rem(m + k, n_member)))

    def sized(ref, send, recv):
        return move(ref, ref, send, recv, (r, far))

    rim_sends = jnp.where(jnp.logical_or(to_high, to_low), n_member, 0)
    pl.semaphore_wait(barrier, n_member - 1 + rim_sends - jnp.where(first_end, 1, 0))

    @pl.when(last_end)
    def _():
        pl.semaphore_signal(far_ready, inc=1, device_id=(r, far), device_id_type=MESH)

    turns = [jnp.where(lower == 0, late, early) for late, early in zip(peers + [far], [far] + peers)]
    for e in turns[:-1]:
        near_copy(e).start()

    @pl.when(jnp.logical_not(first_end))
    def _():
        near_copy(turns[-1]).start()

    @pl.when(to_high)
    def _():
        for k in range(n_member):
            rim_copy(k, 1, m - half, 1).start()

    @pl.when(to_low)
    def _():
        for k in range(n_member):
            rim_copy(k, -1, half + n_member + m, 2).start()

    @pl.when(jnp.logical_not(has_low))
    def _():
        ext[pl.ds(0, half * tiles)] = jnp.zeros((half * tiles, ROWS, TILE), jnp.float32)

    @pl.when(jnp.logical_not(has_high))
    def _():
        ext[pl.ds((half + n_member) * tiles, half * tiles)] = jnp.zeros(
            (half * tiles, ROWS, TILE), jnp.float32
        )

    across = lax.broadcasted_iota(jnp.int32, (ROWS, TILE), 0) < 2
    middle = jnp.where(across, jnp.broadcast_to(ext[base][:, :1], (ROWS, TILE)), 0.0)
    last = ext.shape[0] - 1
    ext[last] = jnp.zeros((ROWS, TILE), jnp.float32)
    sources[last] = source_table(jnp.zeros((ROWS, TILE), jnp.float32), middle)

    def tabulate(first, count):
        @pl.loop(0, count)
        def _(i):
            for t in range(tiles):
                at = first + i * tiles + t
                sources[at] = source_table(ext[at], middle)

    tabulate(base, 1)
    for t in range(tiles):
        own = place_row[:, t * TILE : (t + 1) * TILE]
        for c in range(3):
            tgt[t * 3 + c] = jnp.broadcast_to(own[c : c + 1], (TILE, TILE)).T
        targets[t] = target_table(own - middle[:3])

    def some_pairs(t, tile_ids):
        columns = jnp.concatenate([sources[e] for e in tile_ids], axis=1)
        planes = jnp.dot(targets[t], columns, preferred_element_type=jnp.float32)
        for side, e in enumerate(tile_ids):
            rows = ext[e]
            y1, y2, h, f1, f2, f3 = [jnp.broadcast_to(rows[c : c + 1], (SUB, TILE)) for c in range(6)]
            h2 = h + h
            for b in range(TILE // SUB):
                at = pl.ds(b * SUB, SUB)
                near, image, c, full, mirror = [
                    planes[(b * PLANES + p) * SUB :][:SUB, side * TILE : (side + 1) * TILE]
                    for p in range(PLANES)
                ]
                d1 = tgt[t * 3, at] - y1
                d2 = tgt[t * 3 + 1, at] - y2
                x3 = tgt[t * 3 + 2, at]
                d3 = x3 - h
                w = lax.rsqrt(near)
                p = lax.rsqrt(image)
                w3 = w * w * w
                p2 = p * p
                p3 = p2 * p
                cp3 = c * p3
                alpha = (w + w3) - (p + cp3)
                gamma = cp3 * p2 * mirror
                both = full * (w3 - p3) + gamma
                terms = (f1 * alpha + d1 * both, f2 * alpha + d2 * both, f3 * alpha + d3 * both + h2 * gamma)
                for k in range(3):
                    acc[t * 3 + k, at] = acc[t * 3 + k, at] + terms[k]

    @pl.loop(0, tiles)
    def _(t):
        rows = ext[base + t]
        y1, y2, h, f1, f2, f3 = [jnp.broadcast_to(rows[c : c + 1], (SUB, TILE)) for c in range(6)]
        source = (y1, y2, h, f1, f2, f3, h + h)
        for b in range(TILE // SUB):
            at = pl.ds(b * SUB, SUB)
            terms = pair_terms(tgt[t * 3, at], tgt[t * 3 + 1, at], tgt[t * 3 + 2, at], source)
            for k in range(3):
                acc[t * 3 + k, at] = terms[k]

    first_id = (m * (own_plates * pb)).astype(jnp.float32)
    place = lax.broadcasted_iota(jnp.int32, (hot.shape[1], TILE), 0).astype(jnp.float32)
    slots = [m] + peers
    name_row = lax.broadcasted_iota(jnp.int32, (ROWS, TILE), 0)
    slot_lane = lax.broadcasted_iota(jnp.int32, (ROWS, TILE), 1).astype(jnp.float32)

    def seats(at):
        return jnp.where(place == at, 1.0, 0.0).astype(jnp.bfloat16)

    def find(j):
        for t in range(tiles):
            hot[j, :, t * TILE : (t + 1) * TILE] = seats(ext[(half + slots[j]) * tiles + t][6:7] - first_id)
        names = [jnp.where(name_row == 0, slot_lane, j * tiles + t + 1.0) for t in range(tiles)]
        return lax.dot_general(
            jnp.concatenate(names, axis=1).astype(jnp.bfloat16),
            hot[j],
            (((1,), (1,)), ((), ())),
            preferred_element_type=jnp.float32,
        )

    found[...] = find(0)

    @pl.when(first_end)
    def _():
        pl.semaphore_wait(far_ready, 1)
        near_copy(far).start()

    @pl.when(has_low)
    def _():
        sized(block(0, half), local_sem.at[0], data_sem.at[1]).wait_recv()

    @pl.when(has_high)
    def _():
        sized(block(0, half), local_sem.at[0], data_sem.at[2]).wait_recv()

    for at in [*range(half * tiles), *range((half + n_member) * tiles, 2 * n_member * tiles)]:
        sources[at] = source_table(ext[at], middle)
    sized(block(0, n_member - 1), local_sem.at[0], data_sem.at[0]).wait_recv()

    for e in others:
        for t in range(tiles):
            at = (half + e) * tiles + t
            sources[at] = source_table(ext[at], middle)

    zeros = jnp.zeros((VROWS - 3, TILE), jnp.float32)

    def vel_copy(e):
        return move(vel.at[m], vel.at[m], local_sem.at[3], data_sem.at[3], (r, e))

    blocks = []
    for t in range(tiles):
        for s in range(1, pairs, 2):
            chosen = [jnp.where(k < count_ref[t], list_ref[t, k], last) for k in range(s, min(s + 2, pairs))]
            some_pairs(t, chosen)
        blocks.append([jnp.sum(acc[t * 3 + c].T, axis=0, keepdims=True) for c in range(3)] + [zeros])
    rows = jnp.concatenate([jnp.concatenate(block, axis=0) for block in blocks], axis=1)
    vel[m] = rows
    for e in peers:
        vel_copy(e).start()
    vel_out[...] = rows[:3]

    count = 2 * n_member * tiles
    gather_table(ext, count, table)

    room = own_plates * pb
    far_tiles = [ext[(half + far) * tiles + t] for t in range(tiles)]
    local = jnp.concatenate([v[6:7] for v in far_tiles], axis=0) - first_id
    mine = jnp.logical_and(local >= 0.0, local < float(room))
    counted = jnp.concatenate(
        [mine.astype(jnp.float32), jnp.zeros((2 * SUB - tiles, TILE), jnp.float32)], axis=0
    ).astype(jnp.bfloat16)
    up_to = lax.broadcasted_iota(jnp.int32, (TILE, TILE), 0) <= lax.broadcasted_iota(jnp.int32, (TILE, TILE), 1)
    order_in = jnp.dot(
        counted, jnp.where(up_to, 1.0, 0.0).astype(jnp.bfloat16), preferred_element_type=jnp.float32
    )
    seat = lax.broadcasted_iota(jnp.int32, (TILE, TILE), 0).astype(jnp.float32)
    row = lax.broadcasted_iota(jnp.int32, (ROWS, TILE), 0)
    before = jnp.full((1, 1), -1.0, jnp.float32)
    chosen, columns = [], []
    for t in range(tiles):
        at = jnp.where(mine[t : t + 1], order_in[t : t + 1] + before, -1.0)
        before = before + order_in[t : t + 1, TILE - 1 :]
        chosen.append(jnp.where(seat == at, 1.0, 0.0))
        id_hi, id_lo, _ = split3(jnp.where(mine[t : t + 1], local[t : t + 1], 0.0))
        extra = jnp.where(row == 0, t + 1.0, jnp.where(row == 1, id_hi, jnp.where(row == 2, id_lo, 0.0)))
        columns.append(jnp.concatenate([*split3(far_tiles[t]), extra], axis=0))
    picked = lax.dot_general(
        jnp.concatenate(columns, axis=1).astype(jnp.bfloat16),
        jnp.concatenate(chosen, axis=1).astype(jnp.bfloat16),
        (((1,), (1,)), ((), ())),
        preferred_element_type=jnp.float32,
    )
    label = picked[3 * ROWS : 3 * ROWS + 1]
    far_id = picked[3 * ROWS + 1 : 3 * ROWS + 2] + picked[3 * ROWS + 2 : 3 * ROWS + 3]
    info = jnp.concatenate([v[7:8] for v in far_tiles], axis=0)
    info = jnp.concatenate([info, jnp.zeros((TILE - tiles, TILE), jnp.float32)], axis=0).T
    of_tile = lax.broadcasted_iota(jnp.int32, (2 * SUB, TILE), 0).astype(jnp.float32) + 1.0
    lists = jnp.dot(
        info[: 2 * SUB, : 2 * SUB].astype(jnp.bfloat16),
        jnp.where(of_tile == label, 1.0, 0.0).astype(jnp.bfloat16),
        preferred_element_type=jnp.float32,
    )
    unused = jnp.logical_and(row == 2, label == 0.0)
    parts = [jnp.where(unused, 1.0, picked[:ROWS]), picked[ROWS : 2 * ROWS], picked[2 * ROWS : 3 * ROWS]]
    x3 = (parts[0] + parts[1] + parts[2])[2:3]

    far_vel = jnp.concatenate(gathered_pairs(table, count, lists, parts, x3, pairs) + [zeros], axis=0)

    order = 3 * pb
    total = -(-order // TILE) * TILE
    source = found[...]
    for j in range(1, len(slots)):
        source = source + find(j)

    def spread(v, k, fill):
        v = jnp.concatenate([v, jnp.zeros((v.shape[0], total - v.shape[1]), jnp.float32)], axis=1)
        lane = lax.broadcasted_iota(jnp.int32, v.shape, 1)
        v = jnp.where(jnp.logical_and(lane >= k * pb, lane < (k + 1) * pb), v, fill)
        shifts = [(c - k) * pb % total for c in range(3)]
        return [pltpu.roll(v, shift, 1) if shift else v for shift in shifts]

    body_all = lax.dot_general(
        jnp.where(label == 0.0, 0.0, far_vel).astype(jnp.bfloat16),
        seats(jnp.where(label == 0.0, -1.0, far_id)),
        (((1,), (1,)), ((), ())),
        preferred_element_type=jnp.float32,
    )
    part_of = lax.broadcasted_iota(jnp.int32, (1, total), 1)
    part_of = [part_of < (c + 1) * pb for c in range(3)]
    spans = [slice(k, k + TILE) for k in range(0, total, TILE)]
    from_lane, from_name, body = [], [], []
    for k in range(own_plates):
        table_k = spread(source, k, 0.0)
        table_k = table_k[0] + table_k[1] + table_k[2]
        from_lane += [jnp.broadcast_to(table_k[:1, v].astype(jnp.int32), (ROWS, TILE)) for v in spans]
        from_name += [jnp.broadcast_to(table_k[1:2, v], (ROWS, TILE)) for v in spans]
        fixed = spread(body_all, k, 0.0)
        fixed = fixed[0][0:1] + fixed[1][1:2] + fixed[2][2:3]
        body += [jnp.broadcast_to(fixed[:, v], (ROWS, TILE)) for v in spans]

    def seat(j, body):
        values = jnp.concatenate([vel[slots[j]], jnp.zeros((ROWS - VROWS, blobs), jnp.float32)], axis=0)
        for t in range(tiles):
            tile = values[:, t * TILE : (t + 1) * TILE]
            body = [
                jnp.where(name == j * tiles + t + 1.0, jnp.take_along_axis(tile, at, axis=1), old)
                for name, at, old in zip(from_name, from_lane, body)
            ]
        return body

    body = seat(0, body)

    sized(vel.at[pl.ds(0, n_member - 2)], local_sem.at[3], data_sem.at[3]).wait_recv()

    for j in range(1, len(slots)):
        body = seat(j, body)
    bodies = []
    for k in range(own_plates):
        rows = jnp.concatenate(body[k * len(spans) : (k + 1) * len(spans)], axis=1)
        row = jnp.where(part_of[0], rows[0:1], jnp.where(part_of[1], rows[1:2], rows[2:3]))
        bodies.append(row[:, :order])
    body_out[...] = jnp.concatenate(bodies, axis=0).astype(jnp.bfloat16)

    sized(block(0, n_member - 1), local_sem.at[0], data_sem.at[0]).wait_send()
    sized(vel.at[pl.ds(0, n_member - 2)], local_sem.at[3], data_sem.at[3]).wait_send()

    @pl.when(jnp.logical_or(to_high, to_low))
    def _():
        sized(block(0, n_member), local_sem.at[1], data_sem.at[1]).wait_send()


def finish(vel_ref, body_ref, vel_out, body_out):
    vel_out[...] = vel_ref[...]
    body_out[...] = body_ref[...]


def on_device(n_region, n_member, positions, forces, blob_platelet, blob_rank, owner, pair_list, pair_count, pre):
    blobs = positions.shape[1]
    tiles = blobs // TILE
    own_plates, order, _ = pre.shape
    pb = order // 3
    seats = -(-own_plates * pb // TILE) * TILE
    depth = -(-3 * (2 * n_member * tiles + ROWS) // TILE) * TILE
    far = pl.BlockSpec(memory_space=pltpu.HBM)
    vector = pl.BlockSpec(memory_space=pltpu.VMEM)
    velocity, body_in = pl.pallas_call(
        functools.partial(kernel, n_region, n_member, pb, own_plates),
        out_shape=(
            pltpu.VMEM((3, blobs), jnp.float32),
            pltpu.VMEM((own_plates, order), jnp.bfloat16),
        ),
        in_specs=[far] * 7,
        out_specs=(vector, vector),
        scratch_shapes=[
            pltpu.VMEM((3, blobs), jnp.float32),
            pltpu.VMEM((3, blobs), jnp.float32),
            pltpu.VMEM((1, blobs), jnp.int32),
            pltpu.VMEM((1, blobs), jnp.int32),
            pltpu.SMEM(owner.shape, jnp.int32),
            pltpu.SMEM(pair_list.shape, jnp.int32),
            pltpu.SMEM(pair_count.shape, jnp.int32),
            pltpu.VMEM((2 * n_member * tiles + 1, ROWS, TILE), jnp.float32),
            pltpu.VMEM((2 * n_member * tiles + 1, DEPTH, TILE), jnp.bfloat16),
            pltpu.VMEM((tiles, PLANES * TILE, DEPTH), jnp.bfloat16),
            pltpu.VMEM((3 * tiles, TILE, TILE), jnp.float32),
            pltpu.VMEM((3 * tiles, TILE, TILE), jnp.float32),
            pltpu.VMEM((GATHER * TILE, depth), jnp.bfloat16),
            pltpu.VMEM((n_member, VROWS, blobs), jnp.float32),
            pltpu.VMEM((n_member - 1, seats, blobs), jnp.bfloat16),
            pltpu.VMEM((ROWS, seats), jnp.float32),
            pltpu.SemaphoreType.DMA((7,)),
            pltpu.SemaphoreType.DMA((4,)),
            pltpu.SemaphoreType.REGULAR,
        ],
        compiler_params=pltpu.CompilerParams(collective_id=0, has_side_effects=True),
    )(
        positions,
        forces,
        blob_platelet,
        blob_rank,
        owner,
        pair_list,
        pair_count,
    )
    body_velocity = jnp.einsum("pab,pb->pa", pre, body_in, preferred_element_type=jnp.float32)
    return pl.pallas_call(
        finish,
        out_shape=(
            jax.ShapeDtypeStruct(velocity.shape, jnp.float32),
            jax.ShapeDtypeStruct(body_velocity.shape, jnp.float32),
        ),
        in_specs=[vector, vector],
        out_specs=(vector, vector),
        compiler_params=pltpu.CompilerParams(vmem_limit_bytes=1024 * 1024),
    )(velocity, body_velocity)


def solution(mesh):
    placed = (
        P(None, ("region", "member")),
        P(None, ("region", "member")),
        P(("region", "member")),
        P(("region", "member")),
        P("region"),
        P(("region", "member"), None),
        P(("region", "member")),
        P(("region", "member"), None, None),
    )
    return jax.shard_map(
        functools.partial(on_device, mesh.shape["region"], mesh.shape["member"]),
        mesh=mesh,
        in_specs=placed,
        out_specs=(P(None, ("region", "member")), P(("region", "member"), None)),
        check_vma=False,
    )
```
